256 devices in a mesh: cp: 8 (over x, z_hi), fsdp: 32 (over z_lo, y, core).
Axes of the slice: x: 4, y: 4, z: 8 (z_hi: 2, z_lo: 4; z = z_hi * 4 + z_lo), core: 2. Of those that a mesh axis runs over, the one named last changes fastest.
Arguments:
- hidden: bfloat16 [32, 1024, 16384], P('fsdp', 'cp'), may hold values from -6 to 6
- norm_gain: bfloat16 [16384], P('fsdp'), may hold values from 0.25 to 1.75
- query_weight: bfloat16 [16384, 256], P('fsdp'), may hold values from -0.0625 to 0.0625
- key_weight: bfloat16 [16384, 128], P('fsdp'), may hold values from -0.0625 to 0.0625
- value_weight: bfloat16 [16384, 128], P('fsdp'), may hold values from -0.046875 to 0.046875
- out_weight: bfloat16 [256, 16384], P(None, 'fsdp'), may hold values from -0.75 to 0.75
- doc_lengths: int32 [32, 4], P('fsdp'), may hold values from 1 to 512, 1024 in all within a row
Outputs:
- attention_out: bfloat16 [32, 1024, 16384], P('fsdp', 'cp')
The draws below stay inside these ranges and needn't reach their ends.
Inputs may be any that keep to these rules, and one draw needn't show every extreme that they name: `doc_lengths`: each row holds the lengths of the 4 documents of one sequence in order; they sum to 1024 and the longest is exactly 512.
All inputs are finite; a program needn't handle non-finite values.
Results may differ from the reference program's by a relative error of at most 0.012.
Values may be sent and summed in bfloat16 or wider, within the bound.
A program may use at most 128 MiB of HBM per device.

```python
import math
import jax
import jax.numpy as jnp
import numpy as np
from jax import lax

D = 16384
HD = 128
QH = 2
NDOC = 4
SEQS = 32
SEQLEN = 1024
MOSTDOC = 512


def steps_of(key, extent, pieces, least, largest):
    gain, own = 1.0, jax.random.fold_in(key, 6)
    for dim, blocks in pieces:
        steps = jnp.exp(jax.random.uniform(jax.random.fold_in(own, dim), (blocks,), jnp.float32, least / len(pieces), largest / len(pieces)))
        gain = gain * jnp.repeat(steps, extent[dim] // blocks).reshape([-1 if axis == dim else 1 for axis in range(len(extent))])
    return gain


def split_up(amount, total, limit, slope):
    weights = [(1 << 20) // math.isqrt(standing ** slope) + 1 for standing in range(2, amount + 1)]
    rest, holding = total - limit - (amount - 1), [1] * (amount - 1)
    while rest > 0:
        candidates = [i for i in range(amount - 1) if holding[i] < limit]
        whole, budget = sum([weights[i] for i in candidates]), rest
        for i in candidates:
            more = min(limit - holding[i], max(1, budget * weights[i] // whole), rest)
            holding[i] = holding[i] + more
            rest = rest - more
    return np.array([limit] + holding)


def uneven_parts(rng, amount, total, bound, lean):
    if amount == 2:
        one = jax.random.randint(rng, (), max(1, total - bound), min(bound, total - 1) + 1)
        return jnp.stack([one, total - one])
    sizes = jnp.asarray(split_up(amount, total, bound, lean), jnp.int32)
    pairs = (amount - 1) // 2
    source_of, taker = sizes[1:1 + 2 * pairs:2], sizes[2:2 + 2 * pairs:2]
    room = jnp.minimum(source_of - 1, bound - taker)
    shifted = jax.random.randint(jax.random.fold_in(rng, 1), (pairs,), 0, 1 << 20) % (room + 1)
    sizes = sizes.at[1:1 + 2 * pairs:2].set(source_of - shifted).at[2:2 + 2 * pairs:2].set(taker + shifted)
    return sizes[jax.random.permutation(jax.random.fold_in(rng, 2), amount)]


def noise(own_key, dims, width, most, pieces=(), held_as=jnp.bfloat16):
    factor_of = steps_of(own_key, dims, pieces, -0.22, 0.18) if pieces else 1.0
    array = jax.random.normal(own_key, dims, jnp.float32) * width * factor_of
    return jnp.minimum(jnp.maximum(array, -most), most).astype(held_as)


def setup_inputs(seed: int = 0) -> dict:
    streams_of = jax.random.split(jax.random.key(seed), 8)
    hidden = noise(streams_of[0], (SEQS, SEQLEN, D), 1.0, 6.0, ((0, 32), (1, 8)))
    norm_gain = jnp.clip(1.0 + 0.15 * jax.random.normal(streams_of[1], (D,), jnp.float32), 0.25, 1.75).astype(jnp.bfloat16)
    query_weight = noise(streams_of[2], (D, QH * HD), (D // 2) ** -0.5, 0.0625, ((0, 32),))
    key_weight = noise(streams_of[3], (D, HD), (D // 2) ** -0.5, 0.0625, ((0, 32),))
    value_weight = noise(streams_of[4], (D, HD), D ** -0.5, 0.046875, ((0, 32),))
    out_weight = noise(streams_of[5], (QH * HD, D), (QH * HD // 4) ** -0.5, 0.75, ((1, 32),))
    doc_lengths = jax.vmap(lambda own: uneven_parts(own, NDOC, SEQLEN, MOSTDOC, 2))(jax.random.split(streams_of[6], SEQS)).reshape((SEQS, NDOC)).astype(jnp.int32)
    return dict(hidden=hidden, norm_gain=norm_gain, query_weight=query_weight, key_weight=key_weight, value_weight=value_weight, out_weight=out_weight, doc_lengths=doc_lengths)


EPSILON = 1e-05
THETA = 500000.0

def rounded(values):
    return lax.optimization_barrier(values.astype(jnp.bfloat16))

def doc_tables(lengths, total):
    lengths = lengths.astype(jnp.int32)
    ends = jnp.cumsum(lengths).astype(jnp.int32)
    starts = (ends - lengths).astype(jnp.int32)
    places = jnp.arange(total, dtype=jnp.int32)
    after = (ends[None, :] <= places[:, None]).astype(jnp.int32)
    doc_ids = lax.optimization_barrier(jnp.sum(after, axis=1)).astype(jnp.int32)
    member = (doc_ids[:, None] == jnp.arange(lengths.shape[0], dtype=jnp.int32)[None, :]).astype(jnp.int32)
    offsets = (places - lax.optimization_barrier(jnp.sum(member * starts[None, :], axis=1))).astype(jnp.int32)
    return (doc_ids, offsets)

def rotate(values, offsets):
    head_dim = values.shape[2]
    half = head_dim // 2
    rates = jnp.power(THETA, -2.0 * jnp.arange(half, dtype=jnp.float32) / head_dim)
    angles = offsets.astype(jnp.float32)[:, None] * rates[None, :]
    cosine = jnp.cos(angles)[:, None, :]
    sine = jnp.sin(angles)[:, None, :]
    first = values[:, :, :half]
    second = values[:, :, half:]
    return jnp.concatenate([first * cosine - second * sine, second * cosine + first * sine], axis=2)

def one_sequence(hidden, lengths, norm_gain, query_weight, key_weight, value_weight, out_weight):
    total = hidden.shape[0]
    head_dim = key_weight.shape[1]
    heads = query_weight.shape[1] // head_dim
    doc_ids, offsets = doc_tables(lengths, total)
    tokens = hidden.astype(jnp.float32)
    scaled = tokens * lax.rsqrt(lax.optimization_barrier(jnp.mean(tokens * tokens, axis=1, keepdims=True)) + EPSILON)
    normed = (scaled * norm_gain.astype(jnp.float32)[None, :]).astype(jnp.bfloat16)
    query_raw = jnp.dot(normed, query_weight, preferred_element_type=jnp.float32)
    key_raw = jnp.dot(normed, key_weight, preferred_element_type=jnp.float32)
    value = rounded(jnp.dot(normed, value_weight, preferred_element_type=jnp.float32))
    query = rounded(rotate(query_raw.reshape(total, heads, head_dim), offsets) * head_dim ** (-0.5))
    key = rounded(rotate(key_raw.reshape(total, 1, head_dim), offsets)[:, 0, :])
    scores = jnp.einsum('qhd,kd->hqk', query.astype(jnp.float32), key.astype(jnp.float32))
    places = jnp.arange(total, dtype=jnp.int32)
    allowed = jnp.logical_and(doc_ids[:, None] == doc_ids[None, :], places[None, :] <= places[:, None])
    weights = jnp.where(allowed[None, :, :], jnp.exp(scores), jnp.float32(0.0))
    totals = lax.optimization_barrier(jnp.sum(weights, axis=2))
    weights_rounded = rounded(weights)
    summed = jnp.einsum('hqk,kd->hqd', weights_rounded.astype(jnp.float32), value.astype(jnp.float32))
    attended = (summed / totals[:, :, None]).astype(jnp.bfloat16)
    attended = attended.transpose(1, 0, 2).reshape(total, heads * head_dim)
    return jnp.dot(attended, out_weight, preferred_element_type=jnp.float32).astype(jnp.bfloat16)

def reference(hidden, norm_gain, query_weight, key_weight, value_weight, out_weight, doc_lengths):

    def per_sequence(pair):
        return one_sequence(pair[0], pair[1], norm_gain, query_weight, key_weight, value_weight, out_weight)
    return lax.map(per_sequence, (hidden, doc_lengths))
```

```python
import jax
import jax.numpy as jnp
import numpy as np
from jax import lax
from jax.experimental import pallas as pl
from jax.experimental.pallas import tpu as pltpu
from jax.sharding import PartitionSpec as P

MESH = pl.DeviceIdType.MESH
EPSILON = 1e-05
THETA = 500000.0

ROWS = 128
D = 16384
SHARD = 512
HD = 128
NS = 16
BF = jnp.bfloat16
F32 = jnp.float32

SLOTS = [(0, 0), (3, 0), (1, 0), (0, 3), (0, 1), (3, 3), (1, 3), (3, 1), (1, 1), (2, 0), (0, 2), (2, 3), (2, 1), (3, 2),
         (1, 2), (2, 2)]
SLOT = {o: i for i, o in enumerate(SLOTS)}

ORDER = [(0, (3, 0)), (0, (1, 0)), (1, (0, 3)), (1, (0, 1)), (0, (0, 3)), (0, (0, 1)), (1, (3, 0)), (1, (1, 0)),
         (0, (2, 0)), (1, (0, 2)), (0, (3, 3)), (0, (3, 1)), (1, (3, 3)), (1, (1, 3)), (0, (1, 3)), (0, (1, 1)),
         (1, (3, 1)), (1, (1, 1)), (0, (0, 2)), (1, (2, 0)), (1, (2, 3)), (0, (2, 3)), (0, (2, 1)), (1, (2, 1)),
         (0, (3, 2)), (1, (3, 2)), (0, (1, 2)), (1, (1, 2)), (0, (2, 2)), (1, (2, 2))]


def forwards(half, offset):
    p, q = offset if half == 0 else offset[::-1]
    first, second = ("y", "z") if half == 0 else ("z", "y")
    put = (lambda a, b: (a, b)) if half == 0 else (lambda a, b: (b, a))
    out = []
    if q == 0:
        if p == 0:
            out += [(first + "+", put(3, 0), None), (first + "-", put(1, 0), None)]
        if p == 3:
            out += [(first + "+", put(2, 0), 0)]
        if p == 1:
            out += [(first + "-", put(2, 0), 1)]
        out += [(second + "+", put(p, 3), None), (second + "-", put(p, 1), None)]
    if q == 3:
        out += [(second + "+", put(p, 2), 0)]
    if q == 1:
        out += [(second + "-", put(p, 2), 1)]
    return out


def device(x, y, z, c):
    x, y, z = lax.rem(x + 4, 4), lax.rem(y + 4, 4), lax.rem(z + 8, 8)
    return (x * 2 + z // 4, ((lax.rem(z, 4) * 4) + y) * 2 + c)


def kernel(hid, gain_ref, wq, wk, wv, wo, dl_ref, rates_ref, out,
           hown, wraw, wbuf, xbuf, acc, srx, ptx, prx, kvbuf, wobuf, outv, qbuf, att,
           lsem, hsem, wsem, osem, dsem, ssem, psem, ksem, outsem, send, ksend):
    cp, fs = lax.axis_index("cp"), lax.axis_index("fsdp")
    x, zh = cp // 2, lax.rem(cp, 2)
    c = lax.rem(fs, 2)
    y = lax.rem(fs // 2, 4)
    zl = fs // 8
    z = zh * 4 + zl
    par = lax.rem(x, 2)
    other = 1 - c

    half = pl.multiple_of(par * 256, 256)
    own_w = [
        pltpu.make_async_copy(wq.at[pl.ds(half, 256)], wraw.at[:, pl.ds(0, 256)], lsem.at[0]),
        pltpu.make_async_copy(wk.at[pl.ds(half, 256)], wraw.at[:, pl.ds(256, 128)], lsem.at[1]),
        pltpu.make_async_copy(wv.at[pl.ds(half, 256)], wraw.at[:, pl.ds(384, 128)], lsem.at[2]),
    ]
    own_h = pltpu.make_async_copy(hid, hown, lsem.at[3])
    own_o = pltpu.make_async_copy(wo, wobuf.at[0, 0], lsem.at[4])
    for copy in own_w:
        copy.start()
    own_h.start()
    own_o.start()

    sibling = device(x, y, z, other)
    step_a = 1 - 2 * par
    partners = [(x + step_a), (x - step_a)]
    link = {"y+": device(x, y + 1, z, c), "y-": device(x, y - 1, z, c),
            "z+": device(x, y, z + 1, c), "z-": device(x, y, z - 1, c)}

    barrier = pltpu.get_barrier_semaphore()
    peers = list(link.values()) + [sibling] + [device(p, y, z, other) for p in partners]
    peers += [(lax.rem(cp + d, 8), fs) for d in range(1, 8)]
    for peer in peers:
        pl.semaphore_signal(barrier, inc=1, device_id=peer, device_id_type=MESH)
    pl.semaphore_wait(barrier, len(peers))

    def column(slot, core):
        dy, dz = SLOTS[slot]
        return ((lax.rem(zl + dz, 4) * 4 + lax.rem(y + dy, 4)) * 2 + core) * SHARD

    def send_hidden(pair):
        for s in (2 * pair, 2 * pair + 1):
            for p in range(2):
                plans = [(sibling, 0, other, par), (device(partners[p], y, z, c), 1, c, 1 - par),
                         (device(partners[p], y, z, other), 2, other, 1 - par)]
                for dst, block, core, parity in plans:
                    col = pl.multiple_of(column(s, core) + (parity * 2 + p) * 128, 128)
                    pltpu.make_async_remote_copy(
                        src_ref=hid.at[:, pl.ds(col, 128)],
                        dst_ref=xbuf.at[p, pl.ds(block * 128, 128), pl.ds(s * 128, 128)],
                        send_sem=send.at[0], recv_sem=hsem.at[p, pair], device_id=dst, device_id_type=MESH).start()

    def wait_hidden(p, pair):
        ref = xbuf.at[p, :, pl.ds(pair * 256, 256)]
        pltpu.make_async_copy(ref, ref, hsem.at[p, pair]).wait()

    def w_view(h, slot, part):
        rows, cols = pl.ds(slot * 128, 128), pl.ds(h * 256, 256)
        return wbuf.at[:, rows, cols] if part is None else wbuf.at[part, rows, cols]

    def o_view(h, slot, part):
        rows = pl.ds(0, 256) if part is None else pl.ds(part * 128, 128)
        return wobuf.at[0, slot, rows, pl.ds(h * 256, 256)]

    def relay(view, sem, which, h, offset):
        for name, there, part in forwards(h, offset):
            pltpu.make_async_remote_copy(
                src_ref=view(h, SLOT[offset], part), dst_ref=view(h, SLOT[there], part),
                send_sem=send.at[which], recv_sem=sem.at[h, SLOT[there]],
                device_id=link[name], device_id_type=MESH).start()

    def arrive(view, sem, h, offset):
        ref = view(h, SLOT[offset], None)
        pltpu.make_async_copy(ref, ref, sem.at[h, SLOT[offset]]).wait()

    send_hidden(0)

    for copy in own_w:
        copy.wait()
    gains = gain_ref[...]
    gains = jnp.where(par == 0, gains[:, :256].astype(F32), gains[:, 256:].astype(F32))
    row = lax.broadcasted_iota(jnp.int32, (256, 256), 0)
    col = lax.broadcasted_iota(jnp.int32, (256, 256), 1)
    diagonal = jnp.where(row == col, jnp.broadcast_to(gains, (256, 256)), 0.0).astype(BF)
    scaled = jnp.dot(diagonal, wraw[...], preferred_element_type=F32).astype(BF)
    wbuf[0, 0:128, :] = scaled[:128]
    wbuf[1, 0:128, :] = scaled[128:]
    relay(w_view, wsem, 1, 0, (0, 0))
    relay(w_view, wsem, 1, 1, (0, 0))
    for pair in range(1, 8):
        send_hidden(pair)

    own_h.wait()

    def square(i, total):
        block = hown[:, pl.ds(pl.multiple_of(i * 512, 512), 512)].astype(F32)
        sq = block * block
        return total + (sq[:, :128] + sq[:, 128:256]) + (sq[:, 256:384] + sq[:, 384:])

    total = lax.fori_loop(0, D // 512, square, jnp.zeros((ROWS, 128), F32))
    scale = lax.rsqrt(jnp.sum(total, axis=1, keepdims=True) * (1.0 / D) + EPSILON)
    places = lax.broadcasted_iota(jnp.int32, (ROWS, 128), 0) + cp * ROWS
    starts = jnp.zeros((ROWS, 128), jnp.int32)
    end = dl_ref[0, 0]
    for j in range(1, 4):
        starts = jnp.where(places >= end, end, starts)
        end = end + dl_ref[0, j]
    angles = (places - starts).astype(F32) * rates_ref[...]
    cosine = jnp.cos(angles)
    sine = jnp.sin(angles)
    lane = lax.broadcasted_iota(jnp.int32, (ROWS, 128), 1)
    sine = jnp.where(lane < 64, -sine, sine)

    def rotate(u):
        return u * cosine + pltpu.roll(u, 64, axis=1) * sine

    def contract(pair):
        for p in range(2):
            wait_hidden(p, pair)
            own = []
            for s in (2 * pair, 2 * pair + 1):
                at = pl.multiple_of(column(s, c) + (par * 2 + p) * 128, 128)
                own.append(hown[:, pl.ds(at, 128)])
            weights = wbuf[p, pair * 256:(pair + 1) * 256, :]
            lhs = jnp.concatenate([jnp.concatenate(own, axis=1), xbuf[p, :, pair * 256:(pair + 1) * 256]], axis=0)
            r = jnp.dot(lhs, weights, preferred_element_type=F32)
            for block, at in enumerate((0, 3, 1 + p, 4 + p)):
                piece = r[block * 128:(block + 1) * 128]
                fresh = pair == 0 and (p == 0 or block >= 2)
                acc[at] = piece if fresh else acc[at] + piece

    seen = {(0, (0, 0)), (1, (0, 0))}
    done = 0
    last = max(i for i, (h, o) in enumerate(ORDER) if forwards(h, o))
    for i, (h, o) in enumerate(ORDER):
        arrive(w_view, wsem, h, o)
        relay(w_view, wsem, 1, h, o)
        seen.add((h, o))
        if i == last:
            own_o.wait()
            relay(o_view, osem, 2, 0, (0, 0))
            relay(o_view, osem, 2, 1, (0, 0))
        while done < 8 and all((k, SLOTS[2 * done + e]) in seen for k in range(2) for e in range(2)):
            contract(done)
            done += 1

    def across(slot):
        return pltpu.make_async_remote_copy(
            src_ref=wobuf.at[0, slot], dst_ref=wobuf.at[1, slot], send_sem=send.at[3], recv_sem=dsem.at[slot],
            device_id=sibling, device_id_type=MESH)

    o_seen = {(0, (0, 0)), (1, (0, 0))}

    def take_out(count):
        for h, o in ORDER[len(o_seen) - 2:len(o_seen) - 2 + count]:
            arrive(o_view, osem, h, o)
            relay(o_view, osem, 2, h, o)
            o_seen.add((h, o))
            if (1 - h, o) in o_seen:
                across(SLOT[o]).start()

    to_sibling = pltpu.make_async_remote_copy(
        src_ref=acc.at[pl.ds(3, 3)], dst_ref=srx, send_sem=send.at[4], recv_sem=ssem,
        device_id=sibling, device_id_type=MESH)
    to_sibling.start()
    across(0).start()
    to_sibling.wait_recv()
    for part, cols in ((1, slice(256, 512)), (0, slice(0, 256))):
        for p in range(2):
            ptx[part, p] = (acc[1 + p, :, cols] + srx[1 + p, :, cols]).astype(BF)
            pltpu.make_async_remote_copy(
                src_ref=ptx.at[part, p], dst_ref=prx.at[part, p], send_sem=send.at[5], recv_sem=psem.at[part, p],
                device_id=device(partners[p], y, z, c), device_id_type=MESH).start()

    def finish(part, cols):
        value = acc[0, :, cols] + srx[0, :, cols]
        for p in range(2):
            ref = prx.at[part, p]
            pltpu.make_async_copy(ref, ref, psem.at[part, p]).wait()
            value = value + prx[part, p].astype(F32)
        return value * scale

    kv = finish(1, slice(256, 512))
    kvbuf[512:640, 0:128] = rotate(kv[:, :128]).astype(BF)
    kvbuf[512:640, 128:256] = kv[:, 128:].astype(BF)

    def kv_copy(d):
        return pltpu.make_async_remote_copy(
            src_ref=kvbuf.at[pl.ds(512, 128)], dst_ref=kvbuf.at[pl.ds((4 - d) * ROWS, ROWS)], send_sem=ksend.at[d - 1], recv_sem=ksem.at[d - 1],
            device_id=(lax.rem(cp + d, 8), fs), device_id_type=MESH)

    for d in (1, 3, 2, 4):
        pl.when(cp + d < 8)(kv_copy(d).start)
    take_out(2)

    qs = finish(0, slice(0, 256))
    qbuf[0:128, :] = (rotate(qs[:, :128]) * HD ** -0.5).astype(BF)
    qbuf[128:256, :] = (rotate(qs[:, 128:]) * HD ** -0.5).astype(BF)
    take_out(2)
    for d in (2, 4, 1, 3):
        @pl.when(cp >= d)
        def _():
            kv_copy(d).wait_recv()

        @pl.when(cp < d)
        def _():
            kvbuf[(4 - d) * ROWS:(5 - d) * ROWS, :] = jnp.zeros((ROWS, 256), BF)

    scores = lax.dot_general(qbuf[...], kvbuf[:, :128], (((1,), (1,)), ((), ())), preferred_element_type=F32)
    keys = lax.broadcasted_iota(jnp.int32, (ROWS, 5 * ROWS), 1) + (cp - 4) * ROWS
    allowed = (keys >= starts[:, :1]) & (keys <= places[:, :1])
    e = jnp.where(jnp.concatenate([allowed, allowed], axis=0), jnp.exp(scores), 0.0)
    mixed = jnp.dot(e.astype(BF), kvbuf[:, 128:], preferred_element_type=F32) / jnp.sum(e, axis=1, keepdims=True)
    att[:, 0:128] = mixed[:128].astype(BF)
    att[:, 128:256] = mixed[128:].astype(BF)

    def project(which, slot, core):
        o = jnp.dot(att[...], wobuf[which, slot], preferred_element_type=F32).astype(BF)
        outv[which, slot] = o
        at = pl.multiple_of(column(slot, core), SHARD)
        pltpu.make_async_copy(outv.at[which, slot], out.at[:, pl.ds(at, SHARD)], outsem).start()

    def sibling_out(slot):
        ref = wobuf.at[1, slot]
        pltpu.make_async_copy(ref, ref, dsem.at[slot]).wait()
        project(1, slot, other)

    ready = [s for s in range(NS) if (0, SLOTS[s]) in o_seen and (1, SLOTS[s]) in o_seen]
    projected = set()
    pending = []
    for s in ready:
        project(0, s, c)
        projected.add(s)
        pending.append(s)
    while len(o_seen) < 32:
        take_out(1)
        for s in range(NS):
            if s not in projected and (0, SLOTS[s]) in o_seen and (1, SLOTS[s]) in o_seen:
                project(0, s, c)
                projected.add(s)
                pending.append(s)
        if len(pending) > 2:
            sibling_out(pending.pop(0))
    for s in pending:
        sibling_out(s)

    def drain(ref, sem):
        pltpu.make_async_copy(ref, ref, sem).wait()

    drain(xbuf, send.at[0])
    drain(wbuf.at[:, pl.ds(128, 15 * 128)], send.at[1])
    drain(wobuf.at[0, pl.ds(1, 15)], send.at[2])
    drain(wobuf.at[1], send.at[3])
    drain(srx, send.at[4])
    drain(prx, send.at[5])
    for d in (1, 2, 3, 4):
        pl.when(cp + d < 8)(kv_copy(d).wait_send)
    drain(outv, outsem)


def local(hidden, norm_gain, query_weight, key_weight, value_weight, out_weight, doc_lengths):
    rates = np.power(np.float32(THETA), -2.0 * np.arange(64, dtype=np.float32) / np.float32(128.0)).astype(np.float32)
    rates = jnp.asarray(np.concatenate([rates, rates])[None, :])
    anywhere = pl.BlockSpec(memory_space=pl.ANY)
    vmem = pl.BlockSpec(memory_space=pltpu.VMEM)
    dma = pltpu.SemaphoreType.DMA
    out = pl.pallas_call(
        kernel,
        out_shape=jax.ShapeDtypeStruct((ROWS, D), BF),
        in_specs=[anywhere, vmem, anywhere, anywhere, anywhere, anywhere,
                  pl.BlockSpec(memory_space=pltpu.SMEM), vmem],
        out_specs=anywhere,
        scratch_shapes=[
            pltpu.VMEM((ROWS, D), BF),
            pltpu.VMEM((256, 512), BF),
            pltpu.VMEM((2, NS * 128, 512), BF),
            pltpu.VMEM((2, 384, NS * 128), BF),
            pltpu.VMEM((6, ROWS, 512), F32),
            pltpu.VMEM((3, ROWS, 512), F32),
            pltpu.VMEM((2, 2, ROWS, 256), BF),
            pltpu.VMEM((2, 2, ROWS, 256), BF),
            pltpu.VMEM((5 * ROWS, 256), BF),
            pltpu.VMEM((2, NS, 256, 512), BF),
            pltpu.VMEM((2, NS, ROWS, 512), BF),
            pltpu.VMEM((2 * ROWS, HD), BF),
            pltpu.VMEM((ROWS, 256), BF),
            dma((5,)), dma((2, 8)), dma((2, NS)), dma((2, NS)), dma((NS,)), dma, dma((2, 2)), dma((4,)), dma,
            dma((6,)), dma((4,)),
        ],
        compiler_params=pltpu.CompilerParams(collective_id=0, has_side_effects=True, vmem_limit_bytes=48 << 20),
    )(hidden[0], norm_gain[None, :], query_weight, key_weight, value_weight, out_weight, doc_lengths, rates)
    return out[None]


def solution(mesh):
    in_specs = (
        P("fsdp", "cp", None),
        P("fsdp"),
        P("fsdp", None),
        P("fsdp", None),
        P("fsdp", None),
        P(None, "fsdp"),
        P("fsdp", None),
    )
    out_specs = P("fsdp", "cp", None)
    return jax.shard_map(local, mesh=mesh, in_specs=in_specs, out_specs=out_specs, check_vma=False)
```

```python
import jax
import jax.numpy as jnp
import numpy as np
from jax import lax
from jax.experimental import pallas as pl
from jax.experimental.pallas import tpu as pltpu
from jax.sharding import PartitionSpec as P

MESH = pl.DeviceIdType.MESH
EPSILON = 1e-05
THETA = 500000.0

ROWS = 128
D = 16384
SHARD = 512
HD = 128
NS = 16
BF = jnp.bfloat16
F32 = jnp.float32

SLOTS = [(0, 0), (1, 0), (3, 0), (0, 3), (3, 3), (1, 1), (1, 3), (0, 1), (3, 1), (2, 3), (2, 1), (1, 2), (3, 2), (0, 2),
         (2, 0), (2, 2)]
SLOT = {o: i for i, o in enumerate(SLOTS)}

ORDER = [(0, (1, 0)), (1, (0, 3)), (0, (3, 0)), (1, (1, 0)), (1, (0, 1)), (1, (3, 3)), (1, (1, 3)), (1, (3, 0)),
         (0, (2, 0)), (0, (1, 1)), (1, (0, 2)), (0, (0, 3)), (0, (3, 3)), (1, (1, 1)), (0, (3, 1)), (0, (1, 3)),
         (0, (0, 1)), (0, (2, 3)), (0, (2, 1)), (1, (3, 1)), (1, (2, 3)), (1, (3, 2)), (1, (1, 2)), (1, (2, 1)),
         (0, (1, 2)), (0, (3, 2)), (0, (0, 2)), (1, (2, 0)), (1, (2, 2)), (0, (2, 2))]
OPENING = ((0, "y"), (1, "z"), (0, "z"), (1, "y"))
TAKE = (3, 2, 1, 6)


def forwards(half, offset):
    p, q = offset if half == 0 else offset[::-1]
    first, second = ("y", "z") if half == 0 else ("z", "y")
    put = (lambda a, b: (a, b)) if half == 0 else (lambda a, b: (b, a))
    out = []
    if q == 0:
        if p == 0:
            out += [(first + "+", put(3, 0), None), (first + "-", put(1, 0), None)]
        if p == 3:
            out += [(first + "+", put(2, 0), 0)]
        if p == 1:
            out += [(first + "-", put(2, 0), 1)]
        out += [(second + "+", put(p, 3), None), (second + "-", put(p, 1), None)]
    if q == 3:
        out += [(second + "+", put(p, 2), 0)]
    if q == 1:
        out += [(second + "-", put(p, 2), 1)]
    return out


def device(x, y, z, c):
    x, y, z = lax.rem(x + 4, 4), lax.rem(y + 4, 4), lax.rem(z + 8, 8)
    return (x * 2 + z // 4, ((lax.rem(z, 4) * 4) + y) * 2 + c)


def kernel(hid, gain_hbm, wq, wk, wv, wo, dl_hbm, rates_hbm, out,
           gain_ref, dl_ref, rates_ref, hown, wraw, wbuf, xbuf, acc, srx, ptx, prx, kvbuf, wobuf, qbuf, att,
           lsem, hsem, wsem, osem, dsem, ssem, psem, ksem, send, ksend):
    cp, fs = lax.axis_index("cp"), lax.axis_index("fsdp")
    x, zh = cp // 2, lax.rem(cp, 2)
    c = lax.rem(fs, 2)
    y = lax.rem(fs // 2, 4)
    zl = fs // 8
    z = zh * 4 + zl
    par = lax.rem(x, 2)
    other = 1 - c

    half = pl.multiple_of(par * 256, 256)
    own_w = [
        pltpu.make_async_copy(wq.at[pl.ds(half, 256)], wraw.at[:, pl.ds(0, 256)], lsem.at[0]),
        pltpu.make_async_copy(wk.at[pl.ds(half, 256)], wraw.at[:, pl.ds(256, 128)], lsem.at[1]),
        pltpu.make_async_copy(wv.at[pl.ds(half, 256)], wraw.at[:, pl.ds(384, 128)], lsem.at[2]),
    ]
    own_h = pltpu.make_async_copy(hid, hown, lsem.at[3])
    own_o = pltpu.make_async_copy(wo, wobuf.at[0, 0], lsem.at[4])
    for copy in own_w:
        copy.start()
    small = [pltpu.make_async_copy(gain_hbm, gain_ref, lsem.at[5]), pltpu.make_async_copy(dl_hbm, dl_ref, lsem.at[6]),
             pltpu.make_async_copy(rates_hbm, rates_ref, lsem.at[7])]
    for copy in small:
        copy.start()
    own_h.start()
    own_o.start()

    sibling = device(x, y, z, other)
    step_a = 1 - 2 * par
    partners = [(x + step_a), (x - step_a)]
    link = {"y+": device(x, y + 1, z, c), "y-": device(x, y - 1, z, c),
            "z+": device(x, y, z + 1, c), "z-": device(x, y, z - 1, c)}

    barrier = pltpu.get_barrier_semaphore()
    peers = list(link.values()) + [sibling] + [device(p, y, z, other) for p in partners]
    peers += [(lax.rem(cp + d, 8), fs) for d in range(1, 8)]
    for peer in peers:
        pl.semaphore_signal(barrier, inc=1, device_id=peer, device_id_type=MESH)
    def column(slot, core):
        dy, dz = SLOTS[slot]
        return ((lax.rem(zl + dz, 4) * 4 + lax.rem(y + dy, 4)) * 2 + core) * SHARD

    def send_hidden(pair):
        for s in (2 * pair, 2 * pair + 1):
            for p in range(2):
                plans = [(sibling, 0, other, par), (device(partners[p], y, z, c), 1, c, 1 - par),
                         (device(partners[p], y, z, other), 2, other, 1 - par)]
                for dst, block, core, parity in plans:
                    col = pl.multiple_of(column(s, core) + (parity * 2 + p) * 128, 128)
                    pltpu.make_async_remote_copy(
                        src_ref=hid.at[:, pl.ds(col, 128)],
                        dst_ref=xbuf.at[p, pl.ds(block * 128, 128), pl.ds(s * 128, 128)],
                        send_sem=send.at[0], recv_sem=hsem.at[p, pair], device_id=dst, device_id_type=MESH).start()

    def wait_hidden(p, pair):
        ref = xbuf.at[p, :, pl.ds(pair * 256, 256)]
        pltpu.make_async_copy(ref, ref, hsem.at[p, pair]).wait()

    def w_view(h, slot, part):
        rows, cols = pl.ds(slot * 128, 128), pl.ds(h * 256, 256)
        return wbuf.at[:, rows, cols] if part is None else wbuf.at[part, rows, cols]

    def o_view(h, slot, part):
        rows = pl.ds(0, 256) if part is None else pl.ds(part * 128, 128)
        return wobuf.at[0, slot, rows, pl.ds(h * 256, 256)]

    def relay(view, sem, which, h, offset, axes="yz"):
        for name, there, part in forwards(h, offset):
            if name[0] not in axes:
                continue
            pltpu.make_async_remote_copy(
                src_ref=view(h, SLOT[offset], part), dst_ref=view(h, SLOT[there], part),
                send_sem=send.at[which], recv_sem=sem.at[h, SLOT[there]],
                device_id=link[name], device_id_type=MESH).start()

    def opening(view, sem, which):
        for h, axis in OPENING:
            relay(view, sem, which, h, (0, 0), axis)

    def arrive(view, sem, h, offset):
        ref = view(h, SLOT[offset], None)
        pltpu.make_async_copy(ref, ref, sem.at[h, SLOT[offset]]).wait()

    for copy in own_w + small:
        copy.wait()
    gains = gain_ref[...].reshape(1, 512)
    gains = jnp.where(par == 0, gains[:, :256].astype(F32), gains[:, 256:].astype(F32))
    row = lax.broadcasted_iota(jnp.int32, (256, 256), 0)
    col = lax.broadcasted_iota(jnp.int32, (256, 256), 1)
    diagonal = jnp.where(row == col, jnp.broadcast_to(gains, (256, 256)), 0.0).astype(BF)
    scaled = jnp.dot(diagonal, wraw[...], preferred_element_type=F32).astype(BF)
    wbuf[0, 0:128, :] = scaled[:128]
    wbuf[1, 0:128, :] = scaled[128:]
    pl.semaphore_wait(barrier, len(peers))
    send_hidden(0)
    opening(w_view, wsem, 1)
    for pair in range(1, 8):
        send_hidden(pair)

    own_h.wait()

    def square(i, total):
        block = hown[:, pl.ds(pl.multiple_of(i * 512, 512), 512)].astype(F32)
        sq = block * block
        return total + (sq[:, :128] + sq[:, 128:256]) + (sq[:, 256:384] + sq[:, 384:])

    total = lax.fori_loop(0, D // 512, square, jnp.zeros((ROWS, 128), F32))
    scale = lax.rsqrt(jnp.sum(total, axis=1, keepdims=True) * (1.0 / D) + EPSILON)
    places = lax.broadcasted_iota(jnp.int32, (ROWS, 128), 0) + cp * ROWS
    starts = jnp.zeros((ROWS, 128), jnp.int32)
    end = dl_ref[0, 0]
    for j in range(1, 4):
        starts = jnp.where(places >= end, end, starts)
        end = end + dl_ref[0, j]
    angles = (places - starts).astype(F32) * rates_ref[...]
    cosine = jnp.cos(angles)
    sine = jnp.sin(angles)
    lane = lax.broadcasted_iota(jnp.int32, (ROWS, 128), 1)
    sine = jnp.where(lane < 64, -sine, sine)

    def rotate(u):
        return u * cosine + pltpu.roll(u, 64, axis=1) * sine

    def contract(pair):
        for p in range(2):
            wait_hidden(p, pair)
            own = []
            for s in (2 * pair, 2 * pair + 1):
                at = pl.multiple_of(column(s, c) + (par * 2 + p) * 128, 128)
                own.append(hown[:, pl.ds(at, 128)])
            weights = wbuf[p, pair * 256:(pair + 1) * 256, :]
            lhs = jnp.concatenate([jnp.concatenate(own, axis=1), xbuf[p, :, pair * 256:(pair + 1) * 256]], axis=0)
            r = jnp.dot(lhs, weights, preferred_element_type=F32)
            for block, at in enumerate((0, 3, 1 + p, 4 + p)):
                piece = r[block * 128:(block + 1) * 128]
                fresh = pair == 0 and (p == 0 or block >= 2)
                acc[at] = piece if fresh else acc[at] + piece

    seen = {(0, (0, 0)), (1, (0, 0))}
    done = 0
    last = max(i for i, (h, o) in enumerate(ORDER) if forwards(h, o))
    for i, (h, o) in enumerate(ORDER):
        arrive(w_view, wsem, h, o)
        relay(w_view, wsem, 1, h, o)
        seen.add((h, o))
        if i == last:
            own_o.wait()
            opening(o_view, osem, 2)
        while done < 8 and all((k, SLOTS[2 * done + e]) in seen for k in range(2) for e in range(2)):
            contract(done)
            done += 1

    def across(slot):
        return pltpu.make_async_remote_copy(
            src_ref=wobuf.at[0, slot], dst_ref=wobuf.at[1, slot], send_sem=send.at[3], recv_sem=dsem.at[slot],
            device_id=sibling, device_id_type=MESH)

    o_seen = {(0, (0, 0)), (1, (0, 0))}

    def take_out(count):
        for h, o in ORDER[len(o_seen) - 2:len(o_seen) - 2 + count]:
            arrive(o_view, osem, h, o)
            relay(o_view, osem, 2, h, o)
            o_seen.add((h, o))
            if (1 - h, o) in o_seen:
                across(SLOT[o]).start()

    to_sibling = pltpu.make_async_remote_copy(
        src_ref=acc.at[pl.ds(3, 3)], dst_ref=srx, send_sem=send.at[4], recv_sem=ssem,
        device_id=sibling, device_id_type=MESH)
    to_sibling.start()
    across(0).start()
    to_sibling.wait_recv()
    for part, cols in ((1, slice(256, 512)), (0, slice(0, 256))):
        for p in range(2):
            ptx[part, p] = (acc[1 + p, :, cols] + srx[1 + p, :, cols]).astype(BF)
            pltpu.make_async_remote_copy(
                src_ref=ptx.at[part, p], dst_ref=prx.at[part, p], send_sem=send.at[5], recv_sem=psem.at[part, p],
                device_id=device(partners[p], y, z, c), device_id_type=MESH).start()

    def finish(part, cols):
        value = acc[0, :, cols] + srx[0, :, cols]
        for p in range(2):
            ref = prx.at[part, p]
            pltpu.make_async_copy(ref, ref, psem.at[part, p]).wait()
            value = value + prx[part, p].astype(F32)
        return value * scale

    take_out(TAKE[0])
    take_out(TAKE[1])
    kv = finish(1, slice(256, 512))
    kvbuf[512:640, 0:128] = rotate(kv[:, :128]).astype(BF)
    kvbuf[512:640, 128:256] = kv[:, 128:].astype(BF)

    def kv_copy(d):
        return pltpu.make_async_remote_copy(
            src_ref=kvbuf.at[pl.ds(512, 128)], dst_ref=kvbuf.at[pl.ds((4 - d) * ROWS, ROWS)], send_sem=ksend.at[d - 1], recv_sem=ksem.at[d - 1],
            device_id=(lax.rem(cp + d, 8), fs), device_id_type=MESH)

    for d in (1, 3, 2, 4):
        pl.when(cp + d < 8)(kv_copy(d).start)
    take_out(TAKE[2])

    qs = finish(0, slice(0, 256))
    qbuf[0:128, :] = (rotate(qs[:, :128]) * HD ** -0.5).astype(BF)
    qbuf[128:256, :] = (rotate(qs[:, 128:]) * HD ** -0.5).astype(BF)
    take_out(TAKE[3])
    for d in (2, 4, 1, 3):
        @pl.when(cp >= d)
        def _():
            kv_copy(d).wait_recv()

        @pl.when(cp < d)
        def _():
            kvbuf[(4 - d) * ROWS:(5 - d) * ROWS, :] = jnp.zeros((ROWS, 256), BF)

    scores = lax.dot_general(qbuf[...], kvbuf[:, :128], (((1,), (1,)), ((), ())), preferred_element_type=F32)
    keys = lax.broadcasted_iota(jnp.int32, (ROWS, 5 * ROWS), 1) + (cp - 4) * ROWS
    allowed = (keys >= starts[:, :1]) & (keys <= places[:, :1])
    e = jnp.where(jnp.concatenate([allowed, allowed], axis=0), jnp.exp(scores), 0.0)
    mixed = jnp.dot(e.astype(BF), kvbuf[:, 128:], preferred_element_type=F32) / jnp.sum(e, axis=1, keepdims=True)
    att[:, 0:128] = mixed[:128].astype(BF)
    att[:, 128:256] = mixed[128:].astype(BF)

    def project(which, slot, core):
        o = jnp.dot(att[...], wobuf[which, slot], preferred_element_type=F32).astype(BF)
        out[:, pl.ds(pl.multiple_of(column(slot, core), SHARD), SHARD)] = o

    def sibling_out(slot):
        ref = wobuf.at[1, slot]
        pltpu.make_async_copy(ref, ref, dsem.at[slot]).wait()
        project(1, slot, other)

    ready = [s for s in range(NS) if (0, SLOTS[s]) in o_seen and (1, SLOTS[s]) in o_seen]
    projected = set()
    pending = []
    for s in ready:
        project(0, s, c)
        projected.add(s)
        pending.append(s)
    while len(o_seen) < 32:
        take_out(1)
        for s in range(NS):
            if s not in projected and (0, SLOTS[s]) in o_seen and (1, SLOTS[s]) in o_seen:
                project(0, s, c)
                projected.add(s)
                pending.append(s)
        if len(pending) > 2:
            sibling_out(pending.pop(0))
    for s in pending:
        sibling_out(s)

    def drain(ref, sem):
        pltpu.make_async_copy(ref, ref, sem).wait()

    drain(xbuf, send.at[0])
    drain(wbuf.at[:, pl.ds(128, 15 * 128)], send.at[1])
    drain(wobuf.at[0, pl.ds(1, 15)], send.at[2])
    drain(wobuf.at[1], send.at[3])
    drain(srx, send.at[4])
    drain(prx, send.at[5])
    for d in (1, 2, 3, 4):
        pl.when(cp + d < 8)(kv_copy(d).wait_send)


def local(hidden, norm_gain, query_weight, key_weight, value_weight, out_weight, doc_lengths):
    rates = np.power(np.float32(THETA), -2.0 * np.arange(64, dtype=np.float32) / np.float32(128.0)).astype(np.float32)
    rates = jnp.asarray(np.concatenate([rates, rates])[None, :])
    hbm = pl.BlockSpec(memory_space=pltpu.MemorySpace.HBM)
    dma = pltpu.SemaphoreType.DMA
    out = pl.pallas_call(
        kernel,
        out_shape=jax.ShapeDtypeStruct((ROWS, D), BF),
        in_specs=[hbm] * 8,
        out_specs=pl.BlockSpec(memory_space=pltpu.VMEM),
        scratch_shapes=[
            pltpu.VMEM((512,), BF),
            pltpu.SMEM((1, 4), jnp.int32),
            pltpu.VMEM((1, 128), F32),
            pltpu.VMEM((ROWS, D), BF),
            pltpu.VMEM((256, 512), BF),
            pltpu.VMEM((2, NS * 128, 512), BF),
            pltpu.VMEM((2, 384, NS * 128), BF),
            pltpu.VMEM((6, ROWS, 512), F32),
            pltpu.VMEM((3, ROWS, 512), F32),
            pltpu.VMEM((2, 2, ROWS, 256), BF),
            pltpu.VMEM((2, 2, ROWS, 256), BF),
            pltpu.VMEM((5 * ROWS, 256), BF),
            pltpu.VMEM((2, NS, 256, 512), BF),
            pltpu.VMEM((2 * ROWS, HD), BF),
            pltpu.VMEM((ROWS, 256), BF),
            dma((8,)), dma((2, 8)), dma((2, NS)), dma((2, NS)), dma((NS,)), dma, dma((2, 2)), dma((4,)),
            dma((6,)), dma((4,)),
        ],
        compiler_params=pltpu.CompilerParams(collective_id=0, has_side_effects=True, vmem_limit_bytes=48 << 20),
    )(*[pltpu.with_memory_space_constraint(a, pltpu.MemorySpace.HBM) for a in (hidden[0], norm_gain, query_weight, key_weight, value_weight, out_weight, doc_lengths, rates)])
    return out[None]


def solution(mesh):
    in_specs = (
        P("fsdp", "cp", None),
        P("fsdp"),
        P("fsdp", None),
        P("fsdp", None),
        P("fsdp", None),
        P(None, "fsdp"),
        P("fsdp", None),
    )
    out_specs = P("fsdp", "cp", None)
    return jax.shard_map(local, mesh=mesh, in_specs=in_specs, out_specs=out_specs, check_vma=False)
```

```python
import jax
import jax.numpy as jnp
import numpy as np
from jax import lax
from jax.experimental import pallas as pl
from jax.experimental.pallas import tpu as pltpu
from jax.sharding import PartitionSpec as P

MESH = pl.DeviceIdType.MESH
EPSILON = 1e-05
THETA = 500000.0

ROWS = 128
D = 16384
SHARD = 512
HD = 128
NS = 16
BF = jnp.bfloat16
F32 = jnp.float32

SLOTS = [
    (0, 0), (0, 1), (0, 3), (1, 0), (3, 0), (1, 1), (3, 1), (3, 3), (1, 3), (0, 2), (2, 0), (2, 1), (3, 2), (2, 3),
    (1, 2), (2, 2)
]
SLOT = {o: i for i, o in enumerate(SLOTS)}

PROGRAM = [
    ("p", 0, "y"), ("w", 0, (3, 0)), ("w", 0, (1, 0)), ("w", 1, (0, 1)), ("w", 1, (0, 3)), ("w", 0, (0, 1)), ("w",
    0, (0, 3)), ("w", 1, (1, 0)), ("w", 1, (3, 0)), ("w", 0, (2, 0)), ("w", 1, (0, 2)), ("w", 1, (3, 1)), ("w", 0,
    (1, 1)), ("w", 1, (1, 1)), ("p", 1, "z"), ("w", 1, (1, 3)), ("w", 0, (2, 3)), ("w", 0, (3, 1)), ("w", 0, (3,
    3)), ("w", 1, (3, 3)), ("w", 0, (2, 1)), ("w", 0, (1, 3)), ("w", 0, (0, 2)), ("w", 1, (3, 2)), ("w", 1, (1, 2)),
    ("o", 1, (0, 3)), ("o", 1, (0, 1)), ("o", 0, (1, 0)), ("w", 1, (2, 0)), ("o", 0, (3, 0)), ("p", 1, "y"), ("w",
    1, (2, 1)), ("w", 0, (3, 2)), ("w", 1, (2, 3)), ("w", 0, (1, 2)), ("w", 1, (2, 2)), ("w", 0, (2, 2)), ("c", 0),
    ("p", 0, "z"), ("c", 1), ("c", 2), ("o", 1, (0, 2)), ("o", 0, (2, 0)), ("o", 0, (3, 3)), ("o", 1, (3, 3)), ("c",
    3), ("o", 1, (1, 3)), ("o", 1, (3, 1)), ("o", 1, (3, 0)), ("o", 0, (1, 1)), ("o", 0, (0, 3)), ("o", 1, (1, 1)),
    ("o", 0, (1, 3)), ("o", 0, (0, 1)), ("o", 1, (1, 2)), ("o", 0, (3, 1)), ("o", 1, (3, 2)), ("o", 1, (1, 0)),
    ("o", 0, (2, 3)), ("o", 0, (2, 1)), ("c", 4), ("o", 1, (2, 3)), ("o", 0, (0, 2)), ("o", 0, (3, 2)), ("o", 1, (2,
    1)), ("o", 1, (2, 0)), ("o", 0, (1, 2)), ("o", 1, (2, 2)), ("o", 0, (2, 2))
]
OPENING = ((0, "y"), (1, "z"), (0, "z"), (1, "y"))

def forwards(half, offset):
    p, q = offset if half == 0 else offset[::-1]
    first, second = ("y", "z") if half == 0 else ("z", "y")
    put = (lambda a, b: (a, b)) if half == 0 else (lambda a, b: (b, a))
    out = []
    if q == 0:
        if p == 0:
            out += [(first + "+", put(3, 0), None), (first + "-", put(1, 0), None)]
        if p == 3:
            out += [(first + "+", put(2, 0), 0)]
        if p == 1:
            out += [(first + "-", put(2, 0), 1)]
        out += [(second + "+", put(p, 3), None), (second + "-", put(p, 1), None)]
    if q == 3:
        out += [(second + "+", put(p, 2), 0)]
    if q == 1:
        out += [(second + "-", put(p, 2), 1)]
    return out


def device(x, y, z, c):
    x, y, z = lax.rem(x + 4, 4), lax.rem(y + 4, 4), lax.rem(z + 8, 8)
    return (x * 2 + z // 4, ((lax.rem(z, 4) * 4) + y) * 2 + c)


def kernel(hid, gain_hbm, wq, wk, wv, wo, dl_hbm, rates_hbm, out,
           gain_ref, dl_ref, rates_ref, hown, wraw, wbuf, xbuf, acc, srx, ptx, prx, kvbuf, wobuf, qbuf, att,
           lsem, hsem, wsem, osem, dsem, ssem, psem, ksem, send, ksend):
    cp, fs = lax.axis_index("cp"), lax.axis_index("fsdp")
    x, zh = cp // 2, lax.rem(cp, 2)
    c = lax.rem(fs, 2)
    y = lax.rem(fs // 2, 4)
    zl = fs // 8
    z = zh * 4 + zl
    par = lax.rem(x, 2)
    other = 1 - c

    half = pl.multiple_of(par * 256, 256)
    own_w = [
        pltpu.make_async_copy(wq.at[pl.ds(half, 256)], wraw.at[:, pl.ds(0, 256)], lsem.at[0]),
        pltpu.make_async_copy(wk.at[pl.ds(half, 256)], wraw.at[:, pl.ds(256, 128)], lsem.at[1]),
        pltpu.make_async_copy(wv.at[pl.ds(half, 256)], wraw.at[:, pl.ds(384, 128)], lsem.at[2]),
    ]
    own_h = pltpu.make_async_copy(hid, hown, lsem.at[3])
    own_o = pltpu.make_async_copy(wo, wobuf.at[0, 0], lsem.at[4])
    for copy in own_w:
        copy.start()
    small = [pltpu.make_async_copy(gain_hbm, gain_ref, lsem.at[5]), pltpu.make_async_copy(dl_hbm, dl_ref, lsem.at[6]),
             pltpu.make_async_copy(rates_hbm, rates_ref, lsem.at[7])]
    for copy in small:
        copy.start()
    own_h.start()
    own_o.start()

    sibling = device(x, y, z, other)
    step_a = 1 - 2 * par
    partners = [(x + step_a), (x - step_a)]
    link = {"y+": device(x, y + 1, z, c), "y-": device(x, y - 1, z, c),
            "z+": device(x, y, z + 1, c), "z-": device(x, y, z - 1, c)}

    barrier = pltpu.get_barrier_semaphore()
    peers = list(link.values()) + [sibling] + [device(p, y, z, other) for p in partners]
    peers += [(lax.rem(cp + d, 8), fs) for d in range(1, 8)]
    for peer in peers:
        pl.semaphore_signal(barrier, inc=1, device_id=peer, device_id_type=MESH)
    def column(slot, core):
        dy, dz = SLOTS[slot]
        return ((lax.rem(zl + dz, 4) * 4 + lax.rem(y + dy, 4)) * 2 + core) * SHARD

    def send_hidden(pair):
        for s in (2 * pair, 2 * pair + 1):
            for p in range(2):
                plans = [(sibling, 0, other, par), (device(partners[p], y, z, c), 1, c, 1 - par),
                         (device(partners[p], y, z, other), 2, other, 1 - par)]
                for dst, block, core, parity in plans:
                    col = pl.multiple_of(column(s, core) + (parity * 2 + p) * 128, 128)
                    pltpu.make_async_remote_copy(
                        src_ref=hid.at[:, pl.ds(col, 128)],
                        dst_ref=xbuf.at[p, pl.ds(block * 128, 128), pl.ds(s * 128, 128)],
                        send_sem=send.at[0], recv_sem=hsem.at[p, pair], device_id=dst, device_id_type=MESH).start()

    def wait_hidden(p, pair):
        ref = xbuf.at[p, :, pl.ds(pair * 256, 256)]
        pltpu.make_async_copy(ref, ref, hsem.at[p, pair]).wait()

    def w_view(h, slot, part):
        rows, cols = pl.ds(slot * 128, 128), pl.ds(h * 256, 256)
        return wbuf.at[:, rows, cols] if part is None else wbuf.at[part, rows, cols]

    def o_view(h, slot, part):
        rows = pl.ds(0, 256) if part is None else pl.ds(part * 128, 128)
        return wobuf.at[0, slot, rows, pl.ds(h * 256, 256)]

    def relay(view, sem, which, h, offset, axes="yz"):
        for name, there, part in forwards(h, offset):
            if name[0] not in axes:
                continue
            pltpu.make_async_remote_copy(
                src_ref=view(h, SLOT[offset], part), dst_ref=view(h, SLOT[there], part),
                send_sem=send.at[which], recv_sem=sem.at[h, SLOT[there]],
                device_id=link[name], device_id_type=MESH).start()

    def opening(view, sem, which):
        for h, axis in OPENING:
            relay(view, sem, which, h, (0, 0), axis)

    def arrive(view, sem, h, offset):
        ref = view(h, SLOT[offset], None)
        pltpu.make_async_copy(ref, ref, sem.at[h, SLOT[offset]]).wait()

    for copy in own_w + small:
        copy.wait()
    gains = gain_ref[...].reshape(1, 512)
    gains = jnp.where(par == 0, gains[:, :256].astype(F32), gains[:, 256:].astype(F32))
    row = lax.broadcasted_iota(jnp.int32, (256, 256), 0)
    col = lax.broadcasted_iota(jnp.int32, (256, 256), 1)
    diagonal = jnp.where(row == col, jnp.broadcast_to(gains, (256, 256)), 0.0).astype(BF)
    scaled = jnp.dot(diagonal, wraw[...], preferred_element_type=F32).astype(BF)
    wbuf[0, 0:128, :] = scaled[:128]
    wbuf[1, 0:128, :] = scaled[128:]
    pl.semaphore_wait(barrier, len(peers))
    send_hidden(0)
    opening(w_view, wsem, 1)
    for pair in range(1, 8):
        send_hidden(pair)

    own_h.wait()

    def square(i, total):
        block = hown[:, pl.ds(pl.multiple_of(i * 512, 512), 512)].astype(F32)
        sq = block * block
        return total + (sq[:, :128] + sq[:, 128:256]) + (sq[:, 256:384] + sq[:, 384:])

    total = lax.fori_loop(0, D // 512, square, jnp.zeros((ROWS, 128), F32))
    scale = lax.rsqrt(jnp.sum(total, axis=1, keepdims=True) * (1.0 / D) + EPSILON)
    places = lax.broadcasted_iota(jnp.int32, (ROWS, 128), 0) + cp * ROWS
    starts = jnp.zeros((ROWS, 128), jnp.int32)
    end = dl_ref[0, 0]
    for j in range(1, 4):
        starts = jnp.where(places >= end, end, starts)
        end = end + dl_ref[0, j]
    angles = (places - starts).astype(F32) * rates_ref[...]
    cosine = jnp.cos(angles)
    sine = jnp.sin(angles)
    lane = lax.broadcasted_iota(jnp.int32, (ROWS, 128), 1)
    sine = jnp.where(lane < 64, -sine, sine)

    def rotate(u):
        return u * cosine + pltpu.roll(u, 64, axis=1) * sine

    def contract(pair):
        for p in range(2):
            wait_hidden(p, pair)
            own = []
            for s in (2 * pair, 2 * pair + 1):
                at = pl.multiple_of(column(s, c) + (par * 2 + p) * 128, 128)
                own.append(hown[:, pl.ds(at, 128)])
            weights = wbuf[p, pair * 256:(pair + 1) * 256, :]
            lhs = jnp.concatenate([jnp.concatenate(own, axis=1), xbuf[p, :, pair * 256:(pair + 1) * 256]], axis=0)
            r = jnp.dot(lhs, weights, preferred_element_type=F32)
            for block, at in enumerate((0, 3, 1 + p, 4 + p)):
                piece = r[block * 128:(block + 1) * 128]
                fresh = pair == 0 and (p == 0 or block >= 2)
                acc[at] = piece if fresh else acc[at] + piece

    def across(slot):
        return pltpu.make_async_remote_copy(
            src_ref=wobuf.at[0, slot], dst_ref=wobuf.at[1, slot], send_sem=send.at[3], recv_sem=dsem.at[slot],
            device_id=sibling, device_id_type=MESH)

    def project(which, slot, core):
        o = jnp.dot(att[...], wobuf[which, slot], preferred_element_type=F32).astype(BF)
        out[:, pl.ds(pl.multiple_of(column(slot, core), SHARD), SHARD)] = o

    def sibling_out(slot):
        ref = wobuf.at[1, slot]
        pltpu.make_async_copy(ref, ref, dsem.at[slot]).wait()
        project(1, slot, other)

    to_sibling = pltpu.make_async_remote_copy(
        src_ref=acc.at[pl.ds(3, 3)], dst_ref=srx, send_sem=send.at[4], recv_sem=ssem,
        device_id=sibling, device_id_type=MESH)

    def send_partials():
        to_sibling.wait_recv()
        for part, cols in ((1, slice(256, 512)), (0, slice(0, 256))):
            for p in range(2):
                ptx[part, p] = (acc[1 + p, :, cols] + srx[1 + p, :, cols]).astype(BF)
                pltpu.make_async_remote_copy(
                    src_ref=ptx.at[part, p], dst_ref=prx.at[part, p], send_sem=send.at[5], recv_sem=psem.at[part, p],
                    device_id=device(partners[p], y, z, c), device_id_type=MESH).start()

    def finish(part, cols):
        value = acc[0, :, cols] + srx[0, :, cols]
        for p in range(2):
            ref = prx.at[part, p]
            pltpu.make_async_copy(ref, ref, psem.at[part, p]).wait()
            value = value + prx[part, p].astype(F32)
        return value * scale

    def kv_copy(d):
        return pltpu.make_async_remote_copy(
            src_ref=kvbuf.at[pl.ds(512, 128)], dst_ref=kvbuf.at[pl.ds((4 - d) * ROWS, ROWS)],
            send_sem=ksend.at[d - 1], recv_sem=ksem.at[d - 1],
            device_id=(lax.rem(cp + d, 8), fs), device_id_type=MESH)

    def share_kv():
        kv = finish(1, slice(256, 512))
        kvbuf[512:640, 0:128] = rotate(kv[:, :128]).astype(BF)
        kvbuf[512:640, 128:256] = kv[:, 128:].astype(BF)
        for d in (1, 3, 2, 4):
            pl.when(cp + d < 8)(kv_copy(d).start)

    def make_queries():
        qs = finish(0, slice(0, 256))
        qbuf[0:128, :] = (rotate(qs[:, :128]) * HD ** -0.5).astype(BF)
        qbuf[128:256, :] = (rotate(qs[:, 128:]) * HD ** -0.5).astype(BF)

    def attend():
        for d in (2, 4, 1, 3):
            @pl.when(cp >= d)
            def _():
                kv_copy(d).wait_recv()

            @pl.when(cp < d)
            def _():
                kvbuf[(4 - d) * ROWS:(5 - d) * ROWS, :] = jnp.zeros((ROWS, 256), BF)

        scores = lax.dot_general(qbuf[...], kvbuf[:, :128], (((1,), (1,)), ((), ())), preferred_element_type=F32)
        keys = lax.broadcasted_iota(jnp.int32, (ROWS, 5 * ROWS), 1) + (cp - 4) * ROWS
        allowed = (keys >= starts[:, :1]) & (keys <= places[:, :1])
        e = jnp.where(jnp.concatenate([allowed, allowed], axis=0), jnp.exp(scores), 0.0)
        mixed = jnp.dot(e.astype(BF), kvbuf[:, 128:], preferred_element_type=F32) / jnp.sum(e, axis=1, keepdims=True)
        att[:, 0:128] = mixed[:128].astype(BF)
        att[:, 128:256] = mixed[128:].astype(BF)

    chain = [to_sibling.start, send_partials, share_kv, make_queries, attend]
    seen = {("w", 0, (0, 0)), ("w", 1, (0, 0)), ("o", 0, (0, 0)), ("o", 1, (0, 0))}
    contracted, attended, ready, pending = 0, False, [], []

    def out_ready(slot):
        across(slot).start()
        (pending if attended else ready).append(slot)
        if attended:
            project(0, slot, c)

    for step in PROGRAM:
        if step[0] == "c":
            chain[step[1]]()
            if step[1] == 4:
                attended = True
                for slot in ready:
                    project(0, slot, c)
                pending += ready
        elif step[0] == "p":
            if ("started",) not in seen:
                seen.add(("started",))
                own_o.wait()
                out_ready(0)
            relay(o_view, osem, 2, step[1], (0, 0), step[2])
        else:
            kind, h, o = step
            view, sem, which = (w_view, wsem, 1) if kind == "w" else (o_view, osem, 2)
            arrive(view, sem, h, o)
            relay(view, sem, which, h, o)
            seen.add(step)
            if kind == "o" and (kind, 1 - h, o) in seen:
                out_ready(SLOT[o])
            while contracted < 8 and all(("w", k, SLOTS[2 * contracted + e]) in seen for k in range(2) for e in range(2)):
                contract(contracted)
                contracted += 1
        if attended:
            while len(pending) > 2:
                sibling_out(pending.pop(0))
    for slot in pending:
        sibling_out(slot)

    def drain(ref, sem):
        pltpu.make_async_copy(ref, ref, sem).wait()

    drain(xbuf, send.at[0])
    drain(wbuf.at[:, pl.ds(128, 15 * 128)], send.at[1])
    drain(wobuf.at[0, pl.ds(1, 15)], send.at[2])
    drain(wobuf.at[1], send.at[3])
    drain(srx, send.at[4])
    drain(prx, send.at[5])
    for d in (1, 2, 3, 4):
        pl.when(cp + d < 8)(kv_copy(d).wait_send)


def local(hidden, norm_gain, query_weight, key_weight, value_weight, out_weight, doc_lengths):
    rates = np.power(np.float32(THETA), -2.0 * np.arange(64, dtype=np.float32) / np.float32(128.0)).astype(np.float32)
    rates = jnp.asarray(np.concatenate([rates, rates])[None, :])
    hbm = pl.BlockSpec(memory_space=pltpu.MemorySpace.HBM)
    dma = pltpu.SemaphoreType.DMA
    out = pl.pallas_call(
        kernel,
        out_shape=jax.ShapeDtypeStruct((ROWS, D), BF),
        in_specs=[hbm] * 8,
        out_specs=pl.BlockSpec(memory_space=pltpu.VMEM),
        scratch_shapes=[
            pltpu.VMEM((512,), BF),
            pltpu.SMEM((1, 4), jnp.int32),
            pltpu.VMEM((1, 128), F32),
            pltpu.VMEM((ROWS, D), BF),
            pltpu.VMEM((256, 512), BF),
            pltpu.VMEM((2, NS * 128, 512), BF),
            pltpu.VMEM((2, 384, NS * 128), BF),
            pltpu.VMEM((6, ROWS, 512), F32),
            pltpu.VMEM((3, ROWS, 512), F32),
            pltpu.VMEM((2, 2, ROWS, 256), BF),
            pltpu.VMEM((2, 2, ROWS, 256), BF),
            pltpu.VMEM((5 * ROWS, 256), BF),
            pltpu.VMEM((2, NS, 256, 512), BF),
            pltpu.VMEM((2 * ROWS, HD), BF),
            pltpu.VMEM((ROWS, 256), BF),
            dma((8,)), dma((2, 8)), dma((2, NS)), dma((2, NS)), dma((NS,)), dma, dma((2, 2)), dma((4,)),
            dma((6,)), dma((4,)),
        ],
        compiler_params=pltpu.CompilerParams(collective_id=0, has_side_effects=True, vmem_limit_bytes=48 << 20),
    )(*[pltpu.with_memory_space_constraint(a, pltpu.MemorySpace.HBM) for a in (hidden[0], norm_gain, query_weight, key_weight, value_weight, out_weight, doc_lengths, rates)])
    return out[None]


def solution(mesh):
    in_specs = (
        P("fsdp", "cp", None),
        P("fsdp"),
        P("fsdp", None),
        P("fsdp", None),
        P("fsdp", None),
        P(None, "fsdp"),
        P("fsdp", None),
    )
    out_specs = P("fsdp", "cp", None)
    return jax.shard_map(local, mesh=mesh, in_specs=in_specs, out_specs=out_specs, check_vma=False)
```

```python
import jax
import jax.numpy as jnp
import numpy as np
from jax import lax
from jax.experimental import pallas as pl
from jax.experimental.pallas import tpu as pltpu
from jax.sharding import PartitionSpec as P

MESH = pl.DeviceIdType.MESH
EPSILON = 1e-05
THETA = 500000.0

ROWS = 128
D = 16384
SHARD = 512
HD = 128
NS = 16
W_CUT = 64
O_CUT = 112
BF = jnp.bfloat16
F32 = jnp.float32

SLOTS = [
    (0, 0), (0, 1), (1, 1), (3, 0), (3, 1), (3, 3), (1, 0), (0, 3), (1, 3), (1, 2), (2, 1), (2, 0), (0, 2), (3, 2),
    (2, 3), (2, 2)
]
SLOT = {o: i for i, o in enumerate(SLOTS)}

PROGRAM = [
    ("w", 0, (3, 0)), ("w", 0, (1, 0)), ("w", 1, (0, 1)), ("p", 0, "y"), ("w", 1, (0, 3)), ("w", 0, (2, 0)), ("w",
    0, (0, 1)), ("w", 0, (1, 1)), ("w", 0, (1, 3)), ("w", 1, (1, 1)), ("w", 1, (3, 0)), ("w", 0, (3, 3)), ("w", 1,
    (0, 2)), ("p", 1, "z"), ("w", 0, (3, 1)), ("w", 1, (3, 1)), ("w", 1, (3, 3)), ("w", 1, (1, 0)), ("w", 0, (0,
    3)), ("w", 1, (1, 3)), ("w", 0, (2, 3)), ("w", 0, (1, 2)), ("w", 0, (2, 1)), ("w", 1, (3, 2)), ("w", 1, (1, 2)),
    ("o", 0, (1, 0)), ("o", 0, (3, 0)), ("p", 1, "y"), ("w", 1, (2, 1)), ("o", 1, (0, 3)), ("w", 1, (2, 0)), ("o",
    1, (0, 1)), ("w", 0, (0, 2)), ("w", 0, (3, 2)), ("w", 0, (2, 2)), ("w", 1, (2, 3)), ("w", 1, (2, 2)), ("c", 0),
    ("c", 1), ("o", 0, (2, 0)), ("p", 0, "z"), ("o", 1, (0, 2)), ("o", 1, (3, 3)), ("c", 2), ("o", 0, (3, 3)), ("o",
    0, (3, 1)), ("o", 1, (3, 0)), ("o", 0, (1, 1)), ("o", 1, (1, 3)), ("o", 0, (2, 3)), ("c", 3), ("o", 0, (1, 3)),
    ("o", 1, (1, 1)), ("o", 0, (2, 1)), ("o", 0, (0, 1)), ("o", 1, (1, 0)), ("o", 1, (3, 2)), ("o", 0, (0, 3)),
    ("o", 1, (1, 2)), ("o", 1, (3, 1)), ("c", 4), ("o", 1, (2, 0)), ("o", 1, (2, 3)), ("o", 1, (2, 2)), ("o", 0, (2,
    2)), ("o", 1, (2, 1)), ("o", 0, (1, 2)), ("o", 0, (3, 2)), ("o", 0, (0, 2))
]
OPENING = ((0, "y"), (1, "z"), (0, "z"), (1, "y"))

def forwards(half, offset):
    p, q = offset if half == 0 else offset[::-1]
    first, second = ("y", "z") if half == 0 else ("z", "y")
    put = (lambda a, b: (a, b)) if half == 0 else (lambda a, b: (b, a))
    out = []
    if q == 0:
        if p == 0:
            out += [(first + "+", put(3, 0), None), (first + "-", put(1, 0), None)]
        if p == 3:
            out += [(first + "+", put(2, 0), 0)]
        if p == 1:
            out += [(first + "-", put(2, 0), 1)]
        out += [(second + "+", put(p, 3), None), (second + "-", put(p, 1), None)]
    if q == 3:
        out += [(second + "+", put(p, 2), 0)]
    if q == 1:
        out += [(second + "-", put(p, 2), 1)]
    return out


def device(x, y, z, c):
    x, y, z = lax.rem(x + 4, 4), lax.rem(y + 4, 4), lax.rem(z + 8, 8)
    return (x * 2 + z // 4, ((lax.rem(z, 4) * 4) + y) * 2 + c)


def kernel(hid, gain_hbm, wq, wk, wv, wo, dl_hbm, rates_hbm, out,
           gain_ref, dl_ref, rates_ref, hown, wraw, wbuf, xbuf, acc, srx, ptx, prx, kvbuf, wobuf, qbuf, att,
           lsem, hsem, wsem, osem, dsem, ssem, psem, ksem, send, ksend):
    cp, fs = lax.axis_index("cp"), lax.axis_index("fsdp")
    x, zh = cp // 2, lax.rem(cp, 2)
    c = lax.rem(fs, 2)
    y = lax.rem(fs // 2, 4)
    zl = fs // 8
    z = zh * 4 + zl
    par = lax.rem(x, 2)
    other = 1 - c

    half = pl.multiple_of(par * 256, 256)
    own_w = [
        pltpu.make_async_copy(wq.at[pl.ds(half, 256)], wraw.at[:, pl.ds(0, 256)], lsem.at[0]),
        pltpu.make_async_copy(wk.at[pl.ds(half, 256)], wraw.at[:, pl.ds(256, 128)], lsem.at[1]),
        pltpu.make_async_copy(wv.at[pl.ds(half, 256)], wraw.at[:, pl.ds(384, 128)], lsem.at[2]),
    ]
    own_h = pltpu.make_async_copy(hid, hown, lsem.at[3])
    own_o = pltpu.make_async_copy(wo, wobuf.at[0, 0], lsem.at[4])
    for copy in own_w:
        copy.start()
    small = [pltpu.make_async_copy(gain_hbm, gain_ref, lsem.at[5]), pltpu.make_async_copy(dl_hbm, dl_ref, lsem.at[6]),
             pltpu.make_async_copy(rates_hbm, rates_ref, lsem.at[7])]
    for copy in small:
        copy.start()
    own_h.start()
    own_o.start()

    sibling = device(x, y, z, other)
    step_a = 1 - 2 * par
    partners = [(x + step_a), (x - step_a)]
    link = {"y+": device(x, y + 1, z, c), "y-": device(x, y - 1, z, c),
            "z+": device(x, y, z + 1, c), "z-": device(x, y, z - 1, c)}

    barrier = pltpu.get_barrier_semaphore()
    peers = list(link.values()) + [sibling] + [device(p, y, z, other) for p in partners]
    peers += [(lax.rem(cp + d, 8), fs) for d in range(1, 8)]
    for peer in peers:
        pl.semaphore_signal(barrier, inc=1, device_id=peer, device_id_type=MESH)
    def column(slot, core):
        dy, dz = SLOTS[slot]
        return ((lax.rem(zl + dz, 4) * 4 + lax.rem(y + dy, 4)) * 2 + core) * SHARD

    def send_hidden(pair):
        for s in (2 * pair, 2 * pair + 1):
            for p in range(2):
                plans = [(sibling, 0, other, par), (device(partners[p], y, z, c), 1, c, 1 - par),
                         (device(partners[p], y, z, other), 2, other, 1 - par)]
                for dst, block, core, parity in plans:
                    col = pl.multiple_of(column(s, core) + (parity * 2 + p) * 128, 128)
                    pltpu.make_async_remote_copy(
                        src_ref=hid.at[:, pl.ds(col, 128)],
                        dst_ref=xbuf.at[p, pl.ds(block * 128, 128), pl.ds(s * 128, 128)],
                        send_sem=send.at[0], recv_sem=hsem.at[p, pair], device_id=dst, device_id_type=MESH).start()

    def wait_hidden(p, pair):
        ref = xbuf.at[p, :, pl.ds(pair * 256, 256)]
        pltpu.make_async_copy(ref, ref, hsem.at[p, pair]).wait()

    def w_view(h, slot, part):
        rows = pl.ds(slot * 128 + (0, W_CUT)[h], (W_CUT, 128 - W_CUT)[h])
        return wbuf.at[:, rows] if part is None else wbuf.at[part, rows]

    def o_view(h, slot, part):
        rows = pl.ds((0, O_CUT)[h], (O_CUT, 256 - O_CUT)[h])
        return wobuf.at[0, slot, rows] if part is None else wobuf.at[0, slot, rows, pl.ds(part * 256, 256)]

    def relay(view, sem, which, h, offset, axes="yz"):
        for name, there, part in forwards(h, offset):
            if name[0] not in axes:
                continue
            pltpu.make_async_remote_copy(
                src_ref=view(h, SLOT[offset], part), dst_ref=view(h, SLOT[there], part),
                send_sem=send.at[which], recv_sem=sem.at[h, SLOT[there]],
                device_id=link[name], device_id_type=MESH).start()

    def opening(view, sem, which):
        for h, axis in OPENING:
            relay(view, sem, which, h, (0, 0), axis)

    def arrive(view, sem, h, offset):
        ref = view(h, SLOT[offset], None)
        pltpu.make_async_copy(ref, ref, sem.at[h, SLOT[offset]]).wait()

    for copy in own_w + small:
        copy.wait()
    gains = gain_ref[...].reshape(1, 512)
    gains = jnp.where(par == 0, gains[:, :256].astype(F32), gains[:, 256:].astype(F32))
    row = lax.broadcasted_iota(jnp.int32, (256, 256), 0)
    col = lax.broadcasted_iota(jnp.int32, (256, 256), 1)
    diagonal = jnp.where(row == col, jnp.broadcast_to(gains, (256, 256)), 0.0).astype(BF)
    scaled = jnp.dot(diagonal, wraw[...], preferred_element_type=F32).astype(BF)
    wbuf[0, 0:128, :] = scaled[:128]
    wbuf[1, 0:128, :] = scaled[128:]
    pl.semaphore_wait(barrier, len(peers))
    send_hidden(0)
    opening(w_view, wsem, 1)
    for pair in range(1, 8):
        send_hidden(pair)

    own_h.wait()

    def square(i, total):
        block = hown[:, pl.ds(pl.multiple_of(i * 512, 512), 512)].astype(F32)
        sq = block * block
        return total + (sq[:, :128] + sq[:, 128:256]) + (sq[:, 256:384] + sq[:, 384:])

    total = lax.fori_loop(0, D // 512, square, jnp.zeros((ROWS, 128), F32))
    scale = lax.rsqrt(jnp.sum(total, axis=1, keepdims=True) * (1.0 / D) + EPSILON)
    places = lax.broadcasted_iota(jnp.int32, (ROWS, 128), 0) + cp * ROWS
    starts = jnp.zeros((ROWS, 128), jnp.int32)
    end = dl_ref[0, 0]
    for j in range(1, 4):
        starts = jnp.where(places >= end, end, starts)
        end = end + dl_ref[0, j]
    angles = (places - starts).astype(F32) * rates_ref[...]
    cosine = jnp.cos(angles)
    sine = jnp.sin(angles)
    lane = lax.broadcasted_iota(jnp.int32, (ROWS, 128), 1)
    sine = jnp.where(lane < 64, -sine, sine)

    def rotate(u):
        return u * cosine + pltpu.roll(u, 64, axis=1) * sine

    def contract(pair):
        for p in range(2):
            wait_hidden(p, pair)
            own = []
            for s in (2 * pair, 2 * pair + 1):
                at = pl.multiple_of(column(s, c) + (par * 2 + p) * 128, 128)
                own.append(hown[:, pl.ds(at, 128)])
            weights = wbuf[p, pair * 256:(pair + 1) * 256, :]
            lhs = jnp.concatenate([jnp.concatenate(own, axis=1), xbuf[p, :, pair * 256:(pair + 1) * 256]], axis=0)
            r = jnp.dot(lhs, weights, preferred_element_type=F32)
            for block, at in enumerate((0, 3, 1 + p, 4 + p)):
                piece = r[block * 128:(block + 1) * 128]
                fresh = pair == 0 and (p == 0 or block >= 2)
                acc[at] = piece if fresh else acc[at] + piece

    def across(slot):
        return pltpu.make_async_remote_copy(
            src_ref=wobuf.at[0, slot], dst_ref=wobuf.at[1, slot], send_sem=send.at[3], recv_sem=dsem.at[slot],
            device_id=sibling, device_id_type=MESH)

    def project(which, slot, core):
        o = jnp.dot(att[...], wobuf[which, slot], preferred_element_type=F32).astype(BF)
        out[:, pl.ds(pl.multiple_of(column(slot, core), SHARD), SHARD)] = o

    def sibling_out(slot):
        ref = wobuf.at[1, slot]
        pltpu.make_async_copy(ref, ref, dsem.at[slot]).wait()
        project(1, slot, other)

    to_sibling = pltpu.make_async_remote_copy(
        src_ref=acc.at[pl.ds(3, 3)], dst_ref=srx, send_sem=send.at[4], recv_sem=ssem,
        device_id=sibling, device_id_type=MESH)

    def send_partials():
        to_sibling.wait_recv()
        for part, cols in ((1, slice(256, 512)), (0, slice(0, 256))):
            for p in range(2):
                ptx[part, p] = (acc[1 + p, :, cols] + srx[1 + p, :, cols]).astype(BF)
                pltpu.make_async_remote_copy(
                    src_ref=ptx.at[part, p], dst_ref=prx.at[part, p], send_sem=send.at[5], recv_sem=psem.at[part, p],
                    device_id=device(partners[p], y, z, c), device_id_type=MESH).start()

    def finish(part, cols):
        value = acc[0, :, cols] + srx[0, :, cols]
        for p in range(2):
            ref = prx.at[part, p]
            pltpu.make_async_copy(ref, ref, psem.at[part, p]).wait()
            value = value + prx[part, p].astype(F32)
        return value * scale

    def kv_copy(d):
        return pltpu.make_async_remote_copy(
            src_ref=kvbuf.at[pl.ds(512, 128)], dst_ref=kvbuf.at[pl.ds((4 - d) * ROWS, ROWS)],
            send_sem=ksend.at[d - 1], recv_sem=ksem.at[d - 1],
            device_id=(lax.rem(cp + d, 8), fs), device_id_type=MESH)

    def share_kv():
        kv = finish(1, slice(256, 512))
        kvbuf[512:640, 0:128] = rotate(kv[:, :128]).astype(BF)
        kvbuf[512:640, 128:256] = kv[:, 128:].astype(BF)
        for d in (1, 3, 2, 4):
            pl.when(cp + d < 8)(kv_copy(d).start)

    def make_queries():
        qs = finish(0, slice(0, 256))
        qbuf[0:128, :] = (rotate(qs[:, :128]) * HD ** -0.5).astype(BF)
        qbuf[128:256, :] = (rotate(qs[:, 128:]) * HD ** -0.5).astype(BF)

    def attend():
        for d in (2, 4, 1, 3):
            @pl.when(cp >= d)
            def _():
                kv_copy(d).wait_recv()

            @pl.when(cp < d)
            def _():
                kvbuf[(4 - d) * ROWS:(5 - d) * ROWS, :] = jnp.zeros((ROWS, 256), BF)

        scores = lax.dot_general(qbuf[...], kvbuf[:, :128], (((1,), (1,)), ((), ())), preferred_element_type=F32)
        keys = lax.broadcasted_iota(jnp.int32, (ROWS, 5 * ROWS), 1) + (cp - 4) * ROWS
        allowed = (keys >= starts[:, :1]) & (keys <= places[:, :1])
        e = jnp.where(jnp.concatenate([allowed, allowed], axis=0), jnp.exp(scores), 0.0)
        mixed = jnp.dot(e.astype(BF), kvbuf[:, 128:], preferred_element_type=F32) / jnp.sum(e, axis=1, keepdims=True)
        att[:, 0:128] = mixed[:128].astype(BF)
        att[:, 128:256] = mixed[128:].astype(BF)

    chain = [to_sibling.start, send_partials, share_kv, make_queries, attend]
    seen = {("w", 0, (0, 0)), ("w", 1, (0, 0)), ("o", 0, (0, 0)), ("o", 1, (0, 0))}
    contracted, attended, ready, pending = 0, False, [], []

    def out_ready(slot):
        across(slot).start()
        (pending if attended else ready).append(slot)
        if attended:
            project(0, slot, c)

    for step in PROGRAM:
        if step[0] == "c":
            chain[step[1]]()
            if step[1] == 4:
                attended = True
                for slot in ready:
                    project(0, slot, c)
                pending += ready
        elif step[0] == "p":
            if ("started",) not in seen:
                seen.add(("started",))
                own_o.wait()
                out_ready(0)
            relay(o_view, osem, 2, step[1], (0, 0), step[2])
        else:
            kind, h, o = step
            view, sem, which = (w_view, wsem, 1) if kind == "w" else (o_view, osem, 2)
            arrive(view, sem, h, o)
            relay(view, sem, which, h, o)
            seen.add(step)
            if kind == "o" and (kind, 1 - h, o) in seen:
                out_ready(SLOT[o])
            while contracted < 8 and all(("w", k, SLOTS[2 * contracted + e]) in seen for k in range(2) for e in range(2)):
                contract(contracted)
                contracted += 1
        if attended:
            while len(pending) > 2:
                sibling_out(pending.pop(0))
    for slot in pending:
        sibling_out(slot)

    def drain(ref, sem):
        pltpu.make_async_copy(ref, ref, sem).wait()

    drain(xbuf, send.at[0])
    drain(wbuf.at[:, pl.ds(128, 15 * 128)], send.at[1])
    drain(wobuf.at[0, pl.ds(1, 15)], send.at[2])
    drain(wobuf.at[1], send.at[3])
    drain(srx, send.at[4])
    drain(prx, send.at[5])
    for d in (1, 2, 3, 4):
        pl.when(cp + d < 8)(kv_copy(d).wait_send)


def local(hidden, norm_gain, query_weight, key_weight, value_weight, out_weight, doc_lengths):
    rates = np.power(np.float32(THETA), -2.0 * np.arange(64, dtype=np.float32) / np.float32(128.0)).astype(np.float32)
    rates = jnp.asarray(np.concatenate([rates, rates])[None, :])
    hbm = pl.BlockSpec(memory_space=pltpu.MemorySpace.HBM)
    dma = pltpu.SemaphoreType.DMA
    out = pl.pallas_call(
        kernel,
        out_shape=jax.ShapeDtypeStruct((ROWS, D), BF),
        in_specs=[hbm] * 8,
        out_specs=pl.BlockSpec(memory_space=pltpu.VMEM),
        scratch_shapes=[
            pltpu.VMEM((512,), BF),
            pltpu.SMEM((1, 4), jnp.int32),
            pltpu.VMEM((1, 128), F32),
            pltpu.VMEM((ROWS, D), BF),
            pltpu.VMEM((256, 512), BF),
            pltpu.VMEM((2, NS * 128, 512), BF),
            pltpu.VMEM((2, 384, NS * 128), BF),
            pltpu.VMEM((6, ROWS, 512), F32),
            pltpu.VMEM((3, ROWS, 512), F32),
            pltpu.VMEM((2, 2, ROWS, 256), BF),
            pltpu.VMEM((2, 2, ROWS, 256), BF),
            pltpu.VMEM((5 * ROWS, 256), BF),
            pltpu.VMEM((2, NS, 256, 512), BF),
            pltpu.VMEM((2 * ROWS, HD), BF),
            pltpu.VMEM((ROWS, 256), BF),
            dma((8,)), dma((2, 8)), dma((2, NS)), dma((2, NS)), dma((NS,)), dma, dma((2, 2)), dma((4,)),
            dma((6,)), dma((4,)),
        ],
        compiler_params=pltpu.CompilerParams(collective_id=0, has_side_effects=True, vmem_limit_bytes=48 << 20),
    )(*[pltpu.with_memory_space_constraint(a, pltpu.MemorySpace.HBM) for a in (hidden[0], norm_gain, query_weight, key_weight, value_weight, out_weight, doc_lengths, rates)])
    return out[None]


def solution(mesh):
    in_specs = (
        P("fsdp", "cp", None),
        P("fsdp"),
        P("fsdp", None),
        P("fsdp", None),
        P("fsdp", None),
        P(None, "fsdp"),
        P("fsdp", None),
    )
    out_specs = P("fsdp", "cp", None)
    return jax.shard_map(local, mesh=mesh, in_specs=in_specs, out_specs=out_specs, check_vma=False)
```

```python
import jax
import jax.numpy as jnp
import numpy as np
from jax import lax
from jax.experimental import pallas as pl
from jax.experimental.pallas import tpu as pltpu
from jax.sharding import PartitionSpec as P

MESH = pl.DeviceIdType.MESH
EPSILON = 1e-05
THETA = 500000.0

ROWS = 128
D = 16384
SHARD = 512
HD = 128
NS = 16
W_CUT = 64
O_CUT = 112
BF = jnp.bfloat16
F32 = jnp.float32

SLOTS = [
    (0, 0), (0, 1), (0, 3), (1, 0), (3, 1), (3, 0), (1, 1), (3, 3), (1, 3), (0, 2), (2, 0), (2, 3), (1, 2), (2, 1),
    (3, 2), (2, 2)
]
SLOT = {o: i for i, o in enumerate(SLOTS)}

PROGRAM = [
    ("p", 1, "z"), ("w", 0, (1, 0)), ("w", 1, (0, 3)), ("w", 1, (0, 1)), ("w", 0, (3, 0)), ("w", 0, (0, 1)), ("p",
    0, "y"), ("o", 1, (0, 1)), ("w", 0, (1, 3)), ("w", 1, (0, 2)), ("w", 1, (1, 1)), ("w", 1, (3, 1)), ("w", 0, (2,
    0)), ("w", 0, (0, 3)), ("w", 1, (3, 3)), ("o", 0, (1, 0)), ("w", 1, (1, 0)), ("w", 0, (3, 1)), ("w", 1, (3, 0)),
    ("w", 0, (1, 1)), ("w", 0, (3, 3)), ("w", 1, (1, 3)), ("w", 0, (2, 1)), ("w", 1, (3, 2)), ("w", 0, (2, 3)),
    ("o", 1, (3, 1)), ("w", 1, (1, 2)), ("w", 0, (0, 2)), ("o", 0, (1, 1)), ("o", 0, (3, 0)), ("o", 1, (1, 1)),
    ("w", 1, (2, 0)), ("o", 0, (1, 3)), ("o", 1, (0, 3)), ("w", 1, (2, 3)), ("w", 0, (1, 2)), ("w", 1, (2, 1)),
    ("p", 0, "z"), ("w", 0, (3, 2)), ("w", 0, (2, 2)), ("w", 1, (2, 2)), ("c", 0), ("x", 1, (0, 1)), ("x", 0, (1,
    0)), ("o", 0, (3, 1)), ("p", 1, "y"), ("c", 1), ("o", 0, (0, 1)), ("x", 0, (1, 1)), ("x", 1, (1, 1)), ("o", 0,
    (2, 0)), ("o", 1, (1, 3)), ("o", 1, (0, 2)), ("c", 2), ("x", 1, (3, 1)), ("o", 1, (1, 0)), ("x", 1, (1, 3)),
    ("o", 0, (3, 3)), ("x", 0, (3, 1)), ("o", 0, (1, 2)), ("x", 0, (1, 3)), ("o", 1, (3, 0)), ("x", 0, (3, 0)),
    ("o", 1, (3, 3)), ("o", 0, (0, 3)), ("o", 1, (3, 2)), ("o", 0, (2, 3)), ("x", 0, (0, 1)), ("o", 1, (1, 2)),
    ("x", 1, (1, 0)), ("o", 0, (2, 1)), ("c", 3), ("c", 4), ("o", 1, (2, 3)), ("o", 0, (0, 2)), ("x", 1, (0, 3)),
    ("o", 1, (2, 1)), ("o", 0, (3, 2)), ("o", 1, (2, 2)), ("o", 1, (2, 0)), ("x", 1, (3, 0)), ("x", 0, (0, 3)),
    ("o", 0, (2, 2)), ("x", 1, (3, 3)), ("x", 0, (3, 3))
]
OPENING = ((0, "y"), (1, "z"), (0, "z"), (1, "y"))

def forwards(half, offset):
    p, q = offset if half == 0 else offset[::-1]
    first, second = ("y", "z") if half == 0 else ("z", "y")
    put = (lambda a, b: (a, b)) if half == 0 else (lambda a, b: (b, a))
    out = []
    if q == 0:
        if p == 0:
            out += [(first + "+", put(3, 0), None), (first + "-", put(1, 0), None)]
        if p == 3:
            out += [(first + "+", put(2, 0), 0)]
        if p == 1:
            out += [(first + "-", put(2, 0), 1)]
        out += [(second + "+", put(p, 3), None), (second + "-", put(p, 1), None)]
    if q == 3:
        out += [(second + "+", put(p, 2), 0)]
    if q == 1:
        out += [(second + "-", put(p, 2), 1)]
    return out


def last(offset):
    return 2 in offset


def device(x, y, z, c):
    x, y, z = lax.rem(x + 4, 4), lax.rem(y + 4, 4), lax.rem(z + 8, 8)
    return (x * 2 + z // 4, ((lax.rem(z, 4) * 4) + y) * 2 + c)


def kernel(hid, gain_hbm, wq, wk, wv, wo, dl_hbm, rates_hbm, out,
           gain_ref, dl_ref, rates_ref, hown, wraw, wbuf, xbuf, acc, srx, ptx, prx, kvbuf, wobuf, qbuf, att, stage,
           lsem, hsem, wsem, osem, dsem, asem, ssem, psem, ksem, xsem, send, ksend):
    cp, fs = lax.axis_index("cp"), lax.axis_index("fsdp")
    x, zh = cp // 2, lax.rem(cp, 2)
    c = lax.rem(fs, 2)
    y = lax.rem(fs // 2, 4)
    zl = fs // 8
    z = zh * 4 + zl
    par = lax.rem(x, 2)
    other = 1 - c

    half = pl.multiple_of(par * 256, 256)
    own_w = [
        pltpu.make_async_copy(wq.at[pl.ds(half, 256)], wraw.at[:, pl.ds(0, 256)], lsem.at[0]),
        pltpu.make_async_copy(wk.at[pl.ds(half, 256)], wraw.at[:, pl.ds(256, 128)], lsem.at[1]),
        pltpu.make_async_copy(wv.at[pl.ds(half, 256)], wraw.at[:, pl.ds(384, 128)], lsem.at[2]),
    ]
    own_h = pltpu.make_async_copy(hid, hown, lsem.at[3])
    own_o = pltpu.make_async_copy(wo, wobuf.at[0, 0], lsem.at[4])
    for copy in own_w:
        copy.start()
    small = [pltpu.make_async_copy(gain_hbm, gain_ref, lsem.at[5]), pltpu.make_async_copy(dl_hbm, dl_ref, lsem.at[6]),
             pltpu.make_async_copy(rates_hbm, rates_ref, lsem.at[7])]
    for copy in small:
        copy.start()
    own_h.start()
    own_o.start()

    sibling = device(x, y, z, other)
    step_a = 1 - 2 * par
    partners = [(x + step_a), (x - step_a)]
    link = {"y+": device(x, y + 1, z, c), "y-": device(x, y - 1, z, c),
            "z+": device(x, y, z + 1, c), "z-": device(x, y, z - 1, c)}

    barrier = pltpu.get_barrier_semaphore()
    peers = list(link.values()) + [sibling] + [device(p, y, z, other) for p in partners]
    peers += [(lax.rem(cp + d, 8), fs) for d in range(1, 8)]
    for peer in peers:
        pl.semaphore_signal(barrier, inc=1, device_id=peer, device_id_type=MESH)
    def column(slot, core):
        dy, dz = SLOTS[slot]
        return ((lax.rem(zl + dz, 4) * 4 + lax.rem(y + dy, 4)) * 2 + core) * SHARD

    def send_hidden(pair):
        for s in (2 * pair, 2 * pair + 1):
            for p in range(2):
                plans = [(sibling, 0, other, par), (device(partners[p], y, z, c), 1, c, 1 - par),
                         (device(partners[p], y, z, other), 2, other, 1 - par)]
                for dst, block, core, parity in plans:
                    col = pl.multiple_of(column(s, core) + (parity * 2 + p) * 128, 128)
                    pltpu.make_async_remote_copy(
                        src_ref=hid.at[:, pl.ds(col, 128)],
                        dst_ref=xbuf.at[p, pl.ds(block * 128, 128), pl.ds(s * 128, 128)],
                        send_sem=send.at[0], recv_sem=hsem.at[p, pair], device_id=dst, device_id_type=MESH).start()

    def wait_hidden(p, pair):
        ref = xbuf.at[p, :, pl.ds(pair * 256, 256)]
        pltpu.make_async_copy(ref, ref, hsem.at[p, pair]).wait()

    def w_view(h, slot, part):
        rows = pl.ds(slot * 128 + (0, W_CUT)[h], (W_CUT, 128 - W_CUT)[h])
        return wbuf.at[:, rows] if part is None else wbuf.at[part, rows]

    def o_view(h, slot, part=None):
        rows = pl.ds((0, O_CUT)[h], (O_CUT, 256 - O_CUT)[h])
        if part is None:
            return wobuf.at[0, slot, rows]
        return wobuf.at[0, slot, rows, pl.ds(pl.multiple_of(part * 256, 256), 256)]

    def o_send(name, h, offset, there, part):
        pltpu.make_async_remote_copy(
            src_ref=o_view(h, SLOT[offset], part), dst_ref=o_view(h, SLOT[there], part),
            send_sem=send.at[2], recv_sem=osem.at[h, SLOT[there]], device_id=link[name], device_id_type=MESH).start()

    def relay_out(h, offset, axes="yz"):
        for name, there, part in forwards(h, offset):
            if name[0] not in axes:
                continue
            if not last(there):
                o_send(name, h, offset, there, par)
            elif part is None:
                o_send(name, h, offset, there, None)
            elif last(offset) or part == 0:
                o_send(name, h, offset, there, par if part == 0 else 1 - par)
        if offset != (0, 0) and not last(offset):
            swap = o_view(h, SLOT[offset], par)
            pltpu.make_async_remote_copy(
                src_ref=swap, dst_ref=swap, send_sem=send.at[6], recv_sem=xsem.at[h, SLOT[offset]],
                device_id=device(partners[h], y, z, c), device_id_type=MESH).start()

    def relay_rest(h, offset):
        for name, there, part in forwards(h, offset):
            if last(there) and part == 1:
                o_send(name, h, offset, there, 1 - par)

    def arrive_out(h, offset):
        ref = o_view(h, SLOT[offset], None if last(offset) else 0)
        pltpu.make_async_copy(ref, ref, osem.at[h, SLOT[offset]]).wait()

    def arrive_rest(h, offset):
        ref = o_view(h, SLOT[offset], 0)
        pltpu.make_async_copy(ref, ref, xsem.at[h, SLOT[offset]]).wait()

    def relay(view, sem, which, h, offset, axes="yz"):
        for name, there, part in forwards(h, offset):
            if name[0] not in axes:
                continue
            pltpu.make_async_remote_copy(
                src_ref=view(h, SLOT[offset], part), dst_ref=view(h, SLOT[there], part),
                send_sem=send.at[which], recv_sem=sem.at[h, SLOT[there]],
                device_id=link[name], device_id_type=MESH).start()

    def opening(view, sem, which):
        for h, axis in OPENING:
            relay(view, sem, which, h, (0, 0), axis)

    def arrive(view, sem, h, offset):
        ref = view(h, SLOT[offset], None)
        pltpu.make_async_copy(ref, ref, sem.at[h, SLOT[offset]]).wait()

    for copy in own_w + small:
        copy.wait()
    gains = gain_ref[...].reshape(1, 512)
    gains = jnp.where(par == 0, gains[:, :256].astype(F32), gains[:, 256:].astype(F32))
    row = lax.broadcasted_iota(jnp.int32, (256, 256), 0)
    col = lax.broadcasted_iota(jnp.int32, (256, 256), 1)
    diagonal = jnp.where(row == col, jnp.broadcast_to(gains, (256, 256)), 0.0).astype(BF)
    scaled = jnp.dot(diagonal, wraw[...], preferred_element_type=F32).astype(BF)
    wbuf[0, 0:128, :] = scaled[:128]
    wbuf[1, 0:128, :] = scaled[128:]
    pl.semaphore_wait(barrier, len(peers))
    send_hidden(0)
    opening(w_view, wsem, 1)
    for pair in range(1, 8):
        send_hidden(pair)

    own_h.wait()

    def square(i, total):
        block = hown[:, pl.ds(pl.multiple_of(i * 512, 512), 512)].astype(F32)
        sq = block * block
        return total + (sq[:, :128] + sq[:, 128:256]) + (sq[:, 256:384] + sq[:, 384:])

    total = lax.fori_loop(0, D // 512, square, jnp.zeros((ROWS, 128), F32))
    scale = lax.rsqrt(jnp.sum(total, axis=1, keepdims=True) * (1.0 / D) + EPSILON)
    places = lax.broadcasted_iota(jnp.int32, (ROWS, 128), 0) + cp * ROWS
    starts = jnp.zeros((ROWS, 128), jnp.int32)
    end = dl_ref[0, 0]
    for j in range(1, 4):
        starts = jnp.where(places >= end, end, starts)
        end = end + dl_ref[0, j]
    angles = (places - starts).astype(F32) * rates_ref[...]
    cosine = jnp.cos(angles)
    sine = jnp.sin(angles)
    lane = lax.broadcasted_iota(jnp.int32, (ROWS, 128), 1)
    sine = jnp.where(lane < 64, -sine, sine)

    def rotate(u):
        return u * cosine + pltpu.roll(u, 64, axis=1) * sine

    def contract(pair):
        for p in range(2):
            wait_hidden(p, pair)
            own = []
            for s in (2 * pair, 2 * pair + 1):
                at = pl.multiple_of(column(s, c) + (par * 2 + p) * 128, 128)
                own.append(hown[:, pl.ds(at, 128)])
            weights = wbuf[p, pair * 256:(pair + 1) * 256, :]
            lhs = jnp.concatenate([jnp.concatenate(own, axis=1), xbuf[p, :, pair * 256:(pair + 1) * 256]], axis=0)
            r = jnp.dot(lhs, weights, preferred_element_type=F32)
            for block, at in enumerate((0, 3, 1 + p, 4 + p)):
                piece = r[block * 128:(block + 1) * 128]
                fresh = pair == 0 and (p == 0 or block >= 2)
                acc[at] = piece if fresh else acc[at] + piece

    swap_attended = pltpu.make_async_remote_copy(
        src_ref=att.at[0], dst_ref=att.at[1], send_sem=send.at[7], recv_sem=asem, device_id=sibling, device_id_type=MESH)

    def project(slot):
        o = jnp.dot(att[...].reshape(256, 256), wobuf[0, slot], preferred_element_type=F32).astype(BF)
        cols = pl.ds(pl.multiple_of(column(slot, c), SHARD), SHARD)
        out[:, cols] = o[:128]
        stage[slot] = o[128:]
        pltpu.make_async_remote_copy(
            src_ref=stage.at[slot], dst_ref=out.at[:, cols], send_sem=send.at[3], recv_sem=dsem,
            device_id=sibling, device_id_type=MESH).start()

    to_sibling = pltpu.make_async_remote_copy(
        src_ref=acc.at[pl.ds(3, 3)], dst_ref=srx, send_sem=send.at[4], recv_sem=ssem,
        device_id=sibling, device_id_type=MESH)

    def send_partials():
        to_sibling.wait_recv()
        for part, cols in ((1, slice(256, 512)), (0, slice(0, 256))):
            for p in range(2):
                ptx[part, p] = (acc[1 + p, :, cols] + srx[1 + p, :, cols]).astype(BF)
                pltpu.make_async_remote_copy(
                    src_ref=ptx.at[part, p], dst_ref=prx.at[part, p], send_sem=send.at[5], recv_sem=psem.at[part, p],
                    device_id=device(partners[p], y, z, c), device_id_type=MESH).start()

    def finish(part, cols):
        value = acc[0, :, cols] + srx[0, :, cols]
        for p in range(2):
            ref = prx.at[part, p]
            pltpu.make_async_copy(ref, ref, psem.at[part, p]).wait()
            value = value + prx[part, p].astype(F32)
        return value * scale

    def kv_copy(d):
        return pltpu.make_async_remote_copy(
            src_ref=kvbuf.at[pl.ds(512, 128)], dst_ref=kvbuf.at[pl.ds((4 - d) * ROWS, ROWS)],
            send_sem=ksend.at[d - 1], recv_sem=ksem.at[d - 1],
            device_id=(lax.rem(cp + d, 8), fs), device_id_type=MESH)

    def share_kv():
        kv = finish(1, slice(256, 512))
        kvbuf[512:640, 0:128] = rotate(kv[:, :128]).astype(BF)
        kvbuf[512:640, 128:256] = kv[:, 128:].astype(BF)
        for d in (1, 3, 2, 4):
            pl.when(cp + d < 8)(kv_copy(d).start)

    def make_queries():
        qs = finish(0, slice(0, 256))
        qbuf[0:128, :] = (rotate(qs[:, :128]) * HD ** -0.5).astype(BF)
        qbuf[128:256, :] = (rotate(qs[:, 128:]) * HD ** -0.5).astype(BF)

    def attend():
        for d in (2, 4, 1, 3):
            @pl.when(cp >= d)
            def _():
                kv_copy(d).wait_recv()

            @pl.when(cp < d)
            def _():
                kvbuf[(4 - d) * ROWS:(5 - d) * ROWS, :] = jnp.zeros((ROWS, 256), BF)

        scores = lax.dot_general(qbuf[...], kvbuf[:, :128], (((1,), (1,)), ((), ())), preferred_element_type=F32)
        keys = lax.broadcasted_iota(jnp.int32, (ROWS, 5 * ROWS), 1) + (cp - 4) * ROWS
        allowed = (keys >= starts[:, :1]) & (keys <= places[:, :1])
        e = jnp.where(jnp.concatenate([allowed, allowed], axis=0), jnp.exp(scores), 0.0)
        mixed = jnp.dot(e.astype(BF), kvbuf[:, 128:], preferred_element_type=F32) / jnp.sum(e, axis=1, keepdims=True)
        att[0, :, 0:128] = mixed[:128].astype(BF)
        att[0, :, 128:256] = mixed[128:].astype(BF)
        swap_attended.start()
        swap_attended.wait_recv()

    chain = [to_sibling.start, send_partials, share_kv, make_queries, attend]
    seen = {("w", 0, (0, 0)), ("w", 1, (0, 0)), ("o", 0, (0, 0)), ("o", 1, (0, 0))}
    contracted, attended, ready = 0, False, []

    def out_ready(slot):
        if attended:
            project(slot)
        else:
            ready.append(slot)

    for step in PROGRAM:
        if step[0] == "c":
            chain[step[1]]()
            if step[1] == 4:
                attended = True
                for slot in ready:
                    project(slot)
        elif step[0] == "p":
            if ("started",) not in seen:
                seen.add(("started",))
                own_o.wait()
                out_ready(0)
            relay_out(step[1], (0, 0), step[2])
        else:
            kind, h, o = step
            if kind == "w":
                arrive(w_view, wsem, h, o)
                relay(w_view, wsem, 1, h, o)
            elif kind == "o":
                arrive_out(h, o)
                relay_out(h, o)
            else:
                arrive_rest(h, o)
                relay_rest(h, o)
            seen.add(step)
            if kind == ("o" if last(o) else "x") and (kind, 1 - h, o) in seen:
                out_ready(SLOT[o])
            while contracted < 8 and all(("w", k, SLOTS[2 * contracted + e]) in seen for k in range(2) for e in range(2)):
                contract(contracted)
                contracted += 1

    def drain(ref, sem):
        pltpu.make_async_copy(ref, ref, sem).wait()

    drain(xbuf, send.at[0])
    drain(wbuf.at[:, pl.ds(128, 15 * 128)], send.at[1])
    drain(wobuf.at[0, pl.ds(0, 11)], send.at[2])
    drain(wobuf.at[0, pl.ds(0, 4)], send.at[6])
    drain(stage, send.at[3])
    drain(stage, dsem)
    swap_attended.wait_send()
    drain(srx, send.at[4])
    drain(prx, send.at[5])
    for d in (1, 2, 3, 4):
        pl.when(cp + d < 8)(kv_copy(d).wait_send)


def local(hidden, norm_gain, query_weight, key_weight, value_weight, out_weight, doc_lengths):
    rates = np.power(np.float32(THETA), -2.0 * np.arange(64, dtype=np.float32) / np.float32(128.0)).astype(np.float32)
    rates = jnp.asarray(np.concatenate([rates, rates])[None, :])
    hbm = pl.BlockSpec(memory_space=pltpu.MemorySpace.HBM)
    dma = pltpu.SemaphoreType.DMA
    out = pl.pallas_call(
        kernel,
        out_shape=jax.ShapeDtypeStruct((ROWS, D), BF),
        in_specs=[hbm] * 8,
        out_specs=pl.BlockSpec(memory_space=pltpu.VMEM),
        scratch_shapes=[
            pltpu.VMEM((512,), BF),
            pltpu.SMEM((1, 4), jnp.int32),
            pltpu.VMEM((1, 128), F32),
            pltpu.VMEM((ROWS, D), BF),
            pltpu.VMEM((256, 512), BF),
            pltpu.VMEM((2, NS * 128, 512), BF),
            pltpu.VMEM((2, 384, NS * 128), BF),
            pltpu.VMEM((6, ROWS, 512), F32),
            pltpu.VMEM((3, ROWS, 512), F32),
            pltpu.VMEM((2, 2, ROWS, 256), BF),
            pltpu.VMEM((2, 2, ROWS, 256), BF),
            pltpu.VMEM((5 * ROWS, 256), BF),
            pltpu.VMEM((1, NS, 256, 512), BF),
            pltpu.VMEM((2 * ROWS, HD), BF),
            pltpu.VMEM((2, ROWS, 256), BF),
            pltpu.VMEM((NS, ROWS, 512), BF),
            dma((8,)), dma((2, 8)), dma((2, NS)), dma((2, NS)), dma, dma, dma, dma((2, 2)), dma((4,)),
            dma((2, NS)), dma((8,)), dma((4,)),
        ],
        compiler_params=pltpu.CompilerParams(collective_id=0, has_side_effects=True, vmem_limit_bytes=48 << 20),
    )(*[pltpu.with_memory_space_constraint(a, pltpu.MemorySpace.HBM) for a in (hidden[0], norm_gain, query_weight, key_weight, value_weight, out_weight, doc_lengths, rates)])
    return out[None]


def solution(mesh):
    in_specs = (
        P("fsdp", "cp", None),
        P("fsdp"),
        P("fsdp", None),
        P("fsdp", None),
        P("fsdp", None),
        P(None, "fsdp"),
        P("fsdp", None),
    )
    out_specs = P("fsdp", "cp", None)
    return jax.shard_map(local, mesh=mesh, in_specs=in_specs, out_specs=out_specs, check_vma=False)
```

```python
import jax
import jax.numpy as jnp
import numpy as np
from jax import lax
from jax.experimental import pallas as pl
from jax.experimental.pallas import tpu as pltpu
from jax.sharding import PartitionSpec as P

MESH = pl.DeviceIdType.MESH
EPSILON = 1e-05
THETA = 500000.0

ROWS = 128
D = 16384
SHARD = 512
HD = 128
NS = 16
W_CUT = 64
O_CUT = 112
BF = jnp.bfloat16
F32 = jnp.float32

SLOTS = [
    (0, 0), (0, 1), (0, 3), (1, 0), (3, 1), (3, 0), (1, 1), (3, 3), (1, 3), (0, 2), (2, 0), (2, 3), (1, 2), (2, 1),
    (3, 2), (2, 2)
]
SLOT = {o: i for i, o in enumerate(SLOTS)}

PROGRAM = [
    ("p", 1, "z"), ("w", 0, (1, 0)), ("w", 1, (0, 3)), ("w", 1, (0, 1)), ("w", 0, (3, 0)), ("w", 0, (0, 1)), ("p",
    0, "y"), ("o", 1, (0, 1)), ("w", 0, (1, 3)), ("w", 1, (0, 2)), ("w", 1, (1, 1)), ("w", 1, (3, 1)), ("w", 0, (2,
    0)), ("w", 0, (0, 3)), ("w", 1, (3, 3)), ("o", 0, (1, 0)), ("w", 1, (1, 0)), ("w", 0, (3, 1)), ("w", 1, (3, 0)),
    ("w", 0, (1, 1)), ("w", 0, (3, 3)), ("w", 1, (1, 3)), ("w", 0, (2, 1)), ("w", 1, (3, 2)), ("w", 0, (2, 3)),
    ("o", 1, (3, 1)), ("w", 1, (1, 2)), ("w", 0, (0, 2)), ("o", 0, (1, 1)), ("o", 0, (3, 0)), ("o", 1, (1, 1)),
    ("w", 1, (2, 0)), ("o", 0, (1, 3)), ("o", 1, (0, 3)), ("w", 1, (2, 3)), ("w", 0, (1, 2)), ("w", 1, (2, 1)),
    ("p", 0, "z"), ("w", 0, (3, 2)), ("w", 0, (2, 2)), ("w", 1, (2, 2)), ("c", 0), ("x", 1, (0, 1)), ("x", 0, (1,
    0)), ("o", 0, (3, 1)), ("p", 1, "y"), ("c", 1), ("o", 0, (0, 1)), ("x", 0, (1, 1)), ("x", 1, (1, 1)), ("o", 0,
    (2, 0)), ("o", 1, (1, 3)), ("o", 1, (0, 2)), ("c", 2), ("x", 1, (3, 1)), ("o", 1, (1, 0)), ("x", 1, (1, 3)),
    ("o", 0, (3, 3)), ("x", 0, (3, 1)), ("o", 0, (1, 2)), ("x", 0, (1, 3)), ("o", 1, (3, 0)), ("x", 0, (3, 0)),
    ("o", 1, (3, 3)), ("o", 0, (0, 3)), ("o", 1, (3, 2)), ("o", 0, (2, 3)), ("x", 0, (0, 1)), ("o", 1, (1, 2)),
    ("x", 1, (1, 0)), ("o", 0, (2, 1)), ("c", 3), ("c", 4), ("o", 1, (2, 3)), ("o", 0, (0, 2)), ("x", 1, (0, 3)),
    ("o", 1, (2, 1)), ("o", 0, (3, 2)), ("o", 1, (2, 2)), ("o", 1, (2, 0)), ("x", 1, (3, 0)), ("x", 0, (0, 3)),
    ("o", 0, (2, 2)), ("x", 1, (3, 3)), ("x", 0, (3, 3))
]
OPENING = ((0, "y"), (1, "z"), (0, "z"), (1, "y"))

def forwards(half, offset):
    p, q = offset if half == 0 else offset[::-1]
    first, second = ("y", "z") if half == 0 else ("z", "y")
    put = (lambda a, b: (a, b)) if half == 0 else (lambda a, b: (b, a))
    out = []
    if q == 0:
        if p == 0:
            out += [(first + "+", put(3, 0), None), (first + "-", put(1, 0), None)]
        if p == 3:
            out += [(first + "+", put(2, 0), 0)]
        if p == 1:
            out += [(first + "-", put(2, 0), 1)]
        out += [(second + "+", put(p, 3), None), (second + "-", put(p, 1), None)]
    if q == 3:
        out += [(second + "+", put(p, 2), 0)]
    if q == 1:
        out += [(second + "-", put(p, 2), 1)]
    return out


def last(offset):
    return 2 in offset


def device(x, y, z, c):
    x, y, z = lax.rem(x + 4, 4), lax.rem(y + 4, 4), lax.rem(z + 8, 8)
    return (x * 2 + z // 4, ((lax.rem(z, 4) * 4) + y) * 2 + c)


def kernel(hid, gain_hbm, wq, wk, wv, wo, dl_hbm, rates_hbm, out,
           gain_ref, dl_ref, rates_ref, hown, wraw, wbuf, xbuf, acc, srx, ptx, prx, kvbuf, wobuf, qbuf, att, stage,
           lsem, hsem, wsem, osem, dsem, asem, ssem, psem, ksem, xsem, send, ksend):
    cp, fs = lax.axis_index("cp"), lax.axis_index("fsdp")
    x, zh = cp // 2, lax.rem(cp, 2)
    c = lax.rem(fs, 2)
    y = lax.rem(fs // 2, 4)
    zl = fs // 8
    z = zh * 4 + zl
    par = lax.rem(x, 2)
    other = 1 - c

    half = pl.multiple_of(par * 256, 256)
    own_w = [
        pltpu.make_async_copy(wq.at[pl.ds(half, 256)], wraw.at[:, pl.ds(0, 256)], lsem.at[0]),
        pltpu.make_async_copy(wk.at[pl.ds(half, 256)], wraw.at[:, pl.ds(256, 128)], lsem.at[1]),
        pltpu.make_async_copy(wv.at[pl.ds(half, 256)], wraw.at[:, pl.ds(384, 128)], lsem.at[2]),
    ]
    own_h = pltpu.make_async_copy(hid, hown, lsem.at[3])
    own_o = pltpu.make_async_copy(wo, wobuf.at[0, 0], lsem.at[4])
    for copy in own_w:
        copy.start()
    small = [pltpu.make_async_copy(gain_hbm, gain_ref, lsem.at[5]), pltpu.make_async_copy(dl_hbm, dl_ref, lsem.at[6]),
             pltpu.make_async_copy(rates_hbm, rates_ref, lsem.at[7])]
    for copy in small:
        copy.start()
    own_h.start()
    own_o.start()

    sibling = device(x, y, z, other)
    step_a = 1 - 2 * par
    partners = [(x + step_a), (x - step_a)]
    link = {"y+": device(x, y + 1, z, c), "y-": device(x, y - 1, z, c),
            "z+": device(x, y, z + 1, c), "z-": device(x, y, z - 1, c)}

    barrier = pltpu.get_barrier_semaphore()
    peers = list(link.values()) + [sibling] + [device(p, y, z, other) for p in partners]
    peers += [(lax.rem(cp + d, 8), fs) for d in range(1, 8)]
    for peer in peers:
        pl.semaphore_signal(barrier, inc=1, device_id=peer, device_id_type=MESH)
    def column(slot, core):
        dy, dz = SLOTS[slot]
        return ((lax.rem(zl + dz, 4) * 4 + lax.rem(y + dy, 4)) * 2 + core) * SHARD

    def send_hidden(pair):
        for s in (2 * pair, 2 * pair + 1):
            for p in range(2):
                plans = [(sibling, 0, other, par), (device(partners[p], y, z, c), 1, c, 1 - par),
                         (device(partners[p], y, z, other), 2, other, 1 - par)]
                for dst, block, core, parity in plans:
                    col = pl.multiple_of(column(s, core) + (parity * 2 + p) * 128, 128)
                    pltpu.make_async_remote_copy(
                        src_ref=hid.at[:, pl.ds(col, 128)],
                        dst_ref=xbuf.at[p, pl.ds(block * 128, 128), pl.ds(s * 128, 128)],
                        send_sem=send.at[0], recv_sem=hsem.at[p, pair], device_id=dst, device_id_type=MESH).start()

    def wait_hidden(p, pair):
        ref = xbuf.at[p, :, pl.ds(pair * 256, 256)]
        pltpu.make_async_copy(ref, ref, hsem.at[p, pair]).wait()

    def w_view(h, slot, part):
        rows = pl.ds(slot * 128 + (0, W_CUT)[h], (W_CUT, 128 - W_CUT)[h])
        return wbuf.at[:, rows] if part is None else wbuf.at[part, rows]

    def o_view(h, slot, part=None):
        rows = pl.ds((0, O_CUT)[h], (O_CUT, 256 - O_CUT)[h])
        if part is None:
            return wobuf.at[0, slot, rows]
        return wobuf.at[0, slot, rows, pl.ds(pl.multiple_of(part * 256, 256), 256)]

    def o_send(name, h, offset, there, part):
        pltpu.make_async_remote_copy(
            src_ref=o_view(h, SLOT[offset], part), dst_ref=o_view(h, SLOT[there], part),
            send_sem=send.at[2], recv_sem=osem.at[h, SLOT[there]], device_id=link[name], device_id_type=MESH).start()

    def relay_out(h, offset, axes="yz"):
        for name, there, part in forwards(h, offset):
            if name[0] not in axes:
                continue
            if not last(there):
                o_send(name, h, offset, there, par)
            elif part is None:
                o_send(name, h, offset, there, None)
            elif last(offset) or part == 0:
                o_send(name, h, offset, there, par if part == 0 else 1 - par)
        if offset != (0, 0) and not last(offset):
            swap = o_view(h, SLOT[offset], par)
            pltpu.make_async_remote_copy(
                src_ref=swap, dst_ref=swap, send_sem=send.at[6], recv_sem=xsem.at[h, SLOT[offset]],
                device_id=device(partners[h], y, z, c), device_id_type=MESH).start()

    def relay_rest(h, offset):
        for name, there, part in forwards(h, offset):
            if last(there) and part == 1:
                o_send(name, h, offset, there, 1 - par)

    def arrive_out(h, offset):
        ref = o_view(h, SLOT[offset], None if last(offset) else 0)
        pltpu.make_async_copy(ref, ref, osem.at[h, SLOT[offset]]).wait()

    def arrive_rest(h, offset):
        ref = o_view(h, SLOT[offset], 0)
        pltpu.make_async_copy(ref, ref, xsem.at[h, SLOT[offset]]).wait()

    def relay(view, sem, which, h, offset, axes="yz"):
        for name, there, part in forwards(h, offset):
            if name[0] not in axes:
                continue
            pltpu.make_async_remote_copy(
                src_ref=view(h, SLOT[offset], part), dst_ref=view(h, SLOT[there], part),
                send_sem=send.at[which], recv_sem=sem.at[h, SLOT[there]],
                device_id=link[name], device_id_type=MESH).start()

    def opening(view, sem, which):
        for h, axis in OPENING:
            relay(view, sem, which, h, (0, 0), axis)

    def arrive(view, sem, h, offset):
        ref = view(h, SLOT[offset], None)
        pltpu.make_async_copy(ref, ref, sem.at[h, SLOT[offset]]).wait()

    for copy in own_w + small:
        copy.wait()
    gains = gain_ref[...].reshape(1, 512)
    gains = jnp.where(par == 0, gains[:, :256].astype(F32), gains[:, 256:].astype(F32))
    row = lax.broadcasted_iota(jnp.int32, (256, 256), 0)
    col = lax.broadcasted_iota(jnp.int32, (256, 256), 1)
    diagonal = jnp.where(row == col, jnp.broadcast_to(gains, (256, 256)), 0.0).astype(BF)
    scaled = jnp.dot(diagonal, wraw[...], preferred_element_type=F32).astype(BF)
    wbuf[0, 0:128, :] = scaled[:128]
    wbuf[1, 0:128, :] = scaled[128:]
    pl.semaphore_wait(barrier, len(peers))
    opening(w_view, wsem, 1)
    for pair in range(8):
        send_hidden(pair)

    own_h.wait()

    def square(i, total):
        block = hown[:, pl.ds(pl.multiple_of(i * 512, 512), 512)].astype(F32)
        sq = block * block
        return total + (sq[:, :128] + sq[:, 128:256]) + (sq[:, 256:384] + sq[:, 384:])

    total = lax.fori_loop(0, D // 512, square, jnp.zeros((ROWS, 128), F32))
    scale = lax.rsqrt(jnp.sum(total, axis=1, keepdims=True) * (1.0 / D) + EPSILON)
    places = lax.broadcasted_iota(jnp.int32, (ROWS, 128), 0) + cp * ROWS
    starts = jnp.zeros((ROWS, 128), jnp.int32)
    end = dl_ref[0, 0]
    for j in range(1, 4):
        starts = jnp.where(places >= end, end, starts)
        end = end + dl_ref[0, j]
    angles = (places - starts).astype(F32) * rates_ref[...]
    cosine = jnp.cos(angles)
    sine = jnp.sin(angles)
    lane = lax.broadcasted_iota(jnp.int32, (ROWS, 128), 1)
    sine = jnp.where(lane < 64, -sine, sine)

    def rotate(u):
        return u * cosine + pltpu.roll(u, 64, axis=1) * sine

    def contract(pair):
        for p in range(2):
            wait_hidden(p, pair)
            own = []
            for s in (2 * pair, 2 * pair + 1):
                at = pl.multiple_of(column(s, c) + (par * 2 + p) * 128, 128)
                own.append(hown[:, pl.ds(at, 128)])
            weights = wbuf[p, pair * 256:(pair + 1) * 256, :]
            lhs = jnp.concatenate([jnp.concatenate(own, axis=1), xbuf[p, :, pair * 256:(pair + 1) * 256]], axis=0)
            r = jnp.dot(lhs, weights, preferred_element_type=F32)
            for block, at in enumerate((0, 3, 1 + p, 4 + p)):
                piece = r[block * 128:(block + 1) * 128]
                fresh = pair == 0 and (p == 0 or block >= 2)
                acc[at] = piece if fresh else acc[at] + piece

    swap_attended = pltpu.make_async_remote_copy(
        src_ref=att.at[0], dst_ref=att.at[1], send_sem=send.at[7], recv_sem=asem, device_id=sibling, device_id_type=MESH)

    def project(slot):
        o = jnp.dot(att[...].reshape(256, 256), wobuf[0, slot], preferred_element_type=F32).astype(BF)
        cols = pl.ds(pl.multiple_of(column(slot, c), SHARD), SHARD)
        out[:, cols] = o[:128]
        stage[slot] = o[128:]
        pltpu.make_async_remote_copy(
            src_ref=stage.at[slot], dst_ref=out.at[:, cols], send_sem=send.at[3], recv_sem=dsem,
            device_id=sibling, device_id_type=MESH).start()

    to_sibling = pltpu.make_async_remote_copy(
        src_ref=acc.at[pl.ds(3, 3)], dst_ref=srx, send_sem=send.at[4], recv_sem=ssem,
        device_id=sibling, device_id_type=MESH)

    def send_partials():
        to_sibling.wait_recv()
        for part, cols in ((1, slice(256, 512)), (0, slice(0, 256))):
            for p in range(2):
                ptx[part, p] = (acc[1 + p, :, cols] + srx[1 + p, :, cols]).astype(BF)
                pltpu.make_async_remote_copy(
                    src_ref=ptx.at[part, p], dst_ref=prx.at[part, p], send_sem=send.at[5], recv_sem=psem.at[part, p],
                    device_id=device(partners[p], y, z, c), device_id_type=MESH).start()

    def finish(part, cols):
        value = acc[0, :, cols] + srx[0, :, cols]
        for p in range(2):
            ref = prx.at[part, p]
            pltpu.make_async_copy(ref, ref, psem.at[part, p]).wait()
            value = value + prx[part, p].astype(F32)
        return value * scale

    def kv_copy(d):
        return pltpu.make_async_remote_copy(
            src_ref=kvbuf.at[pl.ds(512, 128)], dst_ref=kvbuf.at[pl.ds((4 - d) * ROWS, ROWS)],
            send_sem=ksend.at[d - 1], recv_sem=ksem.at[d - 1],
            device_id=(lax.rem(cp + d, 8), fs), device_id_type=MESH)

    def share_kv():
        kv = finish(1, slice(256, 512))
        kvbuf[512:640, 0:128] = rotate(kv[:, :128]).astype(BF)
        kvbuf[512:640, 128:256] = kv[:, 128:].astype(BF)
        for d in (1, 3, 2, 4):
            pl.when(cp + d < 8)(kv_copy(d).start)

    def make_queries():
        qs = finish(0, slice(0, 256))
        qbuf[0:128, :] = (rotate(qs[:, :128]) * HD ** -0.5).astype(BF)
        qbuf[128:256, :] = (rotate(qs[:, 128:]) * HD ** -0.5).astype(BF)

    def attend():
        for d in (2, 4, 1, 3):
            @pl.when(cp >= d)
            def _():
                kv_copy(d).wait_recv()

            @pl.when(cp < d)
            def _():
                kvbuf[(4 - d) * ROWS:(5 - d) * ROWS, :] = jnp.zeros((ROWS, 256), BF)

        scores = lax.dot_general(qbuf[...], kvbuf[:, :128], (((1,), (1,)), ((), ())), preferred_element_type=F32)
        keys = lax.broadcasted_iota(jnp.int32, (ROWS, 5 * ROWS), 1) + (cp - 4) * ROWS
        allowed = (keys >= starts[:, :1]) & (keys <= places[:, :1])
        e = jnp.where(jnp.concatenate([allowed, allowed], axis=0), jnp.exp(scores), 0.0)
        mixed = jnp.dot(e.astype(BF), kvbuf[:, 128:], preferred_element_type=F32) / jnp.sum(e, axis=1, keepdims=True)
        att[0, :, 0:128] = mixed[:128].astype(BF)
        att[0, :, 128:256] = mixed[128:].astype(BF)
        swap_attended.start()
        swap_attended.wait_recv()

    chain = [to_sibling.start, send_partials, share_kv, make_queries, attend]
    seen = {("w", 0, (0, 0)), ("w", 1, (0, 0)), ("o", 0, (0, 0)), ("o", 1, (0, 0))}
    contracted, attended, ready = 0, False, []

    def out_ready(slot):
        if attended:
            project(slot)
        else:
            ready.append(slot)

    for step in PROGRAM:
        if step[0] == "c":
            chain[step[1]]()
            if step[1] == 4:
                attended = True
                for slot in ready:
                    project(slot)
        elif step[0] == "p":
            if ("started",) not in seen:
                seen.add(("started",))
                own_o.wait()
                out_ready(0)
            relay_out(step[1], (0, 0), step[2])
        else:
            kind, h, o = step
            if kind == "w":
                arrive(w_view, wsem, h, o)
                relay(w_view, wsem, 1, h, o)
            elif kind == "o":
                arrive_out(h, o)
                relay_out(h, o)
            else:
                arrive_rest(h, o)
                relay_rest(h, o)
            seen.add(step)
            if kind == ("o" if last(o) else "x") and (kind, 1 - h, o) in seen:
                out_ready(SLOT[o])
            while contracted < 8 and all(("w", k, SLOTS[2 * contracted + e]) in seen for k in range(2) for e in range(2)):
                contract(contracted)
                contracted += 1

    def drain(ref, sem):
        pltpu.make_async_copy(ref, ref, sem).wait()

    drain(xbuf, send.at[0])
    drain(wbuf.at[:, pl.ds(128, 15 * 128)], send.at[1])
    drain(wobuf.at[0, pl.ds(0, 11)], send.at[2])
    drain(wobuf.at[0, pl.ds(0, 4)], send.at[6])
    drain(stage, send.at[3])
    drain(stage, dsem)
    swap_attended.wait_send()
    drain(srx, send.at[4])
    drain(prx, send.at[5])
    for d in (1, 2, 3, 4):
        pl.when(cp + d < 8)(kv_copy(d).wait_send)


def local(hidden, norm_gain, query_weight, key_weight, value_weight, out_weight, doc_lengths):
    rates = np.power(np.float32(THETA), -2.0 * np.arange(64, dtype=np.float32) / np.float32(128.0)).astype(np.float32)
    rates = jnp.asarray(np.concatenate([rates, rates])[None, :])
    hbm = pl.BlockSpec(memory_space=pltpu.MemorySpace.HBM)
    dma = pltpu.SemaphoreType.DMA
    out = pl.pallas_call(
        kernel,
        out_shape=jax.ShapeDtypeStruct((ROWS, D), BF),
        in_specs=[hbm] * 8,
        out_specs=pl.BlockSpec(memory_space=pltpu.VMEM),
        scratch_shapes=[
            pltpu.VMEM((512,), BF),
            pltpu.SMEM((1, 4), jnp.int32),
            pltpu.VMEM((1, 128), F32),
            pltpu.VMEM((ROWS, D), BF),
            pltpu.VMEM((256, 512), BF),
            pltpu.VMEM((2, NS * 128, 512), BF),
            pltpu.VMEM((2, 384, NS * 128), BF),
            pltpu.VMEM((6, ROWS, 512), F32),
            pltpu.VMEM((3, ROWS, 512), F32),
            pltpu.VMEM((2, 2, ROWS, 256), BF),
            pltpu.VMEM((2, 2, ROWS, 256), BF),
            pltpu.VMEM((5 * ROWS, 256), BF),
            pltpu.VMEM((1, NS, 256, 512), BF),
            pltpu.VMEM((2 * ROWS, HD), BF),
            pltpu.VMEM((2, ROWS, 256), BF),
            pltpu.VMEM((NS, ROWS, 512), BF),
            dma((8,)), dma((2, 8)), dma((2, NS)), dma((2, NS)), dma, dma, dma, dma((2, 2)), dma((4,)),
            dma((2, NS)), dma((8,)), dma((4,)),
        ],
        compiler_params=pltpu.CompilerParams(collective_id=0, has_side_effects=True, vmem_limit_bytes=48 << 20),
    )(*[pltpu.with_memory_space_constraint(a, pltpu.MemorySpace.HBM) for a in (hidden[0], norm_gain, query_weight, key_weight, value_weight, out_weight, doc_lengths, rates)])
    return out[None]


def solution(mesh):
    in_specs = (
        P("fsdp", "cp", None),
        P("fsdp"),
        P("fsdp", None),
        P("fsdp", None),
        P("fsdp", None),
        P(None, "fsdp"),
        P("fsdp", None),
    )
    out_specs = P("fsdp", "cp", None)
    return jax.shard_map(local, mesh=mesh, in_specs=in_specs, out_specs=out_specs, check_vma=False)
```
